32 devices in a mesh: grp: 2 (over y), ep: 8 (over z, x), seq: 1, rep: 2 (over core).
Axes of the slice: x: 2, y: 2, z: 4, core: 2. Of those that a mesh axis runs over, the one named last changes fastest.
Arguments:
- hidden_in: bfloat16 [1024, 2048], P(('grp', 'ep', 'rep'), 'seq'), parts along dimension 0, may hold values from -64 to 64
- row_counts: int32 [32], P(('grp', 'ep', 'rep')), parts along dimension 0, may hold values from 24 to 32, as said below
- qkv_new: bfloat16 [1024, 3, 2048], P(('grp', 'ep', 'rep')), parts along dimension 0, may hold values from -6 to 6
- cache_len: int32 [16, 64], P('grp', ('rep', 'seq')), parts along dimension 0, may hold values from 1 to 128, as said below
- kv_cache: bfloat16 [2, 16, 64, 128, 2048], P(None, 'grp', ('rep', 'seq'), None, 'ep'), parts along dimension 1, may hold values from -128 to 128
- w_out: bfloat16 [2048, 2048], P('ep', 'seq'), may hold values from -0.125 to 0.125
- moe_gain: float32 [2048], replicated, may hold values from 0.1 to 1.9
- w_in: bfloat16 [16, 2048, 2, 1408], P(('ep', 'rep'), None, None, 'seq'), may hold values from -0.125 to 0.125
- w_down: bfloat16 [16, 1408, 2048], P(('ep', 'rep'), 'seq'), may hold values from -0.15625 to 0.15625
- route_ids: int32 [1024, 6], P(('grp', 'ep', 'rep')), parts along dimension 0, may hold values from 0 to 15, all different within a row; in each aligned block of 32 rows (0 to 31, 32 to 63, ...) at most 24 rows name the same one
- route_weight: bfloat16 [1024, 6], P(('grp', 'ep', 'rep')), parts along dimension 0, may hold values from 0.049804688 to 0.44921875
Outputs:
- mixed: bfloat16 [1024, 2048], P(('grp', 'ep', 'rep'), 'seq'), parts along dimension 0
The draws below stay inside these ranges and needn't reach their ends.
There are 2 independent parts, one for each index of `grp`. The reference program is written for one: setup_inputs(seed, part) draws one part's arguments, and reference() takes and returns one part's arrays. A program takes and returns all parts, laid end to end along the dimension named above; an argument that names none is the same for every part. Nothing has to cross between parts.
Inputs may be any that keep to these rules, and one draw needn't show every extreme that they name: The first row_counts[b] slots of block b are live; some block is full. `cache_len`: some row has 128 cached positions. `route_ids`: a row's 6 experts differ; among the 32 rows of one block no expert is named by more than 24 rows, and in some block one is named by exactly 24.
All inputs are finite; a program needn't handle non-finite values.
Results may differ from the reference program's by a relative error of at most 0.0053.
Values may be sent and summed in bfloat16 or wider, within the bound.
A program may use at most 192 MiB of HBM per device.

```python
import math
import jax
import jax.numpy as jnp
import numpy as np
from jax import lax

D = 2048
FF = 1408
HEADS = 16
HEAD_DIM = 128
TOPK = 6
RB = 32
L = 128
ROWS = 512
EXPERTS = 16
CAP = 24
N_EP = 8
N_REP = 2


def make_lengths(key):
    part_keys = jax.random.split(jax.random.fold_in(key, 5), 2)
    lengths = jax.random.randint(part_keys[0], (ROWS,), 1, L + 1)
    longest_row = jax.random.randint(part_keys[1], (), 0, ROWS)
    return jnp.where(jnp.arange(ROWS) == longest_row, L, lengths).astype(jnp.int32)


def make_fresh(key):
    fresh_key = jax.random.fold_in(key, 7)
    drawn = jax.random.truncated_normal(fresh_key, -6.0, 6.0, (ROWS, 3, HEADS * HEAD_DIM), jnp.float32)
    return drawn


def draw_hidden_in(key, part):
    part_keys = jax.random.split(jax.random.fold_in(key, 11), 2)
    base_draw = jax.random.truncated_normal(part_keys[0], -6.0, 6.0, (ROWS, D), jnp.float32)
    column_scale = jnp.exp(jax.random.uniform(part_keys[1], (D,), jnp.float32, 0.0, math.log(10.0))) / 4.0
    column_ramp = 1.0 + 2.0 * jnp.arange(D, dtype=jnp.float32) / D
    drawn = base_draw * column_scale * jnp.sqrt(column_ramp)
    return jnp.clip(drawn, -60.0, 60.0).astype(jnp.bfloat16)


def draw_row_counts(key, part):
    part_keys = jax.random.split(jax.random.fold_in(key, 3), 2)
    blocks = N_EP * N_REP
    counts = jax.random.randint(part_keys[0], (blocks,), RB - RB // 4, RB + 1)
    full_block = jax.random.randint(part_keys[1], (), 0, blocks)
    return jnp.where(jnp.arange(blocks) == full_block, RB, counts).astype(jnp.int32)


def draw_qkv_new(key, part):
    return make_fresh(key).astype(jnp.bfloat16)


def draw_cache_len(key, part):
    return make_lengths(key).reshape(N_EP, N_REP * RB)


def draw_kv_cache(key, part):
    head_width = HEADS * HEAD_DIM
    part_keys = jax.random.split(jax.random.fold_in(key, 9), 2)
    cache_keys = jax.random.truncated_normal(part_keys[0], -6.0, 6.0, (ROWS, L, head_width), jnp.float32)
    cache_values = 2.0 * jax.random.truncated_normal(part_keys[1], -6.0, 6.0, (ROWS, L, head_width), jnp.float32)
    stacked = jnp.stack([cache_keys, cache_values]).reshape(2, N_EP, N_REP * RB, L, head_width)
    return jnp.clip(stacked, -128.0, 128.0).astype(jnp.bfloat16)


def level_of(key, shape, shards, least, high):
    factor_of, own = 1.0, jax.random.fold_in(key, 6)
    for dim, blocks in shards:
        steps = jnp.exp(jax.random.uniform(jax.random.fold_in(own, dim), (blocks,), jnp.float32, least / len(shards), high / len(shards)))
        factor_of = factor_of * jnp.repeat(steps, shape[dim] // blocks).reshape([-1 if axis == dim else 1 for axis in range(len(shape))])
    return factor_of


def shared_out(key, own, number, rows, number_of, top, limit, slope):
    ranking = jax.random.permutation(key, number_of)
    packed, usual = portions_of(number_of, rows * top, limit, slope, True), portions_of(number_of, rows * top, limit, slope, False)
    places = jnp.arange(number_of)

    def named(tallies, turn):
        used = int((tallies > 0).sum())
        fixed = max(1, used // 4)
        moved = fixed + (places - fixed + turn * (used - fixed)) % max(1, number_of - fixed)
        return jnp.zeros((number_of,), jnp.int32).at[ranking[jnp.where(places < fixed, places, moved)]].set(jnp.asarray(tallies, jnp.int32))

    tallies = jnp.where(number % 4 == 0, named(packed, number // 4), named(usual, number - number // 4 - 1))
    mixed = jax.random.permutation(jax.random.fold_in(own, 3), number_of)
    source_of, taker = mixed[0:number_of // 2 * 2:2], mixed[1:number_of // 2 * 2:2]
    margin = jnp.minimum(tallies[source_of] - 1, limit - tallies[taker]) // 2
    margin = jnp.where((source_of == ranking[0]) | (taker == ranking[0]) | (tallies[taker] == 0), 0, jnp.maximum(margin, 0))
    moved = jax.random.randint(jax.random.fold_in(own, 4), (number_of // 2,), 0, 1 << 20) % (margin + 1)
    tallies = tallies.at[source_of].add(-moved).at[taker].add(moved)
    items = jnp.searchsorted(jnp.cumsum(tallies), jnp.arange(rows * top), side="right").astype(jnp.int32)
    listing = items.reshape(top, rows).T
    listing = listing[jax.random.permutation(jax.random.fold_in(own, 1), rows)]
    turn = jax.random.randint(jax.random.fold_in(own, 2), (rows, 1), 0, top)
    return jnp.take_along_axis(listing, (jnp.arange(top)[None, :] + turn) % top, axis=1)


def portions_of(count, total, limit, slope, full):
    weights = [(1 << 20) // math.isqrt(rank ** slope) + 1 for rank in range(1, count + 1)]
    largest = limit if full else min(limit, max(-(-total // count), total * weights[0] // sum(weights)))
    least = 1 if total - largest >= count - 1 else 0
    given, rest = [largest] + [least] * (count - 1), total - largest - least * (count - 1)
    while rest > 0:
        free = [i for i in range(1, count) if given[i] < largest] or [i for i in range(1, count) if given[i] < limit]
        mass, remaining = sum([weights[i] for i in free]), rest
        for i in free:
            more = min(limit - given[i], max(1, remaining * weights[i] // mass), rest)
            given[i] = given[i] + more
            rest = rest - more
    return np.array(given)


def scatter_about(rng, dims, deviation, limit, cuts=(), kind=jnp.bfloat16):
    values = deviation * jax.random.normal(rng, dims, jnp.float32)
    if cuts:
        values = values * level_of(rng, dims, cuts, -0.22, 0.18)
    return jnp.clip(values, -limit, limit).astype(kind)


def setup_inputs(seed: int = 0, part: int = 0) -> dict:
    seeds = jax.random.split(jax.random.key(seed), 12)
    own_keys = jax.random.split(jax.random.fold_in(seeds[11], part), 12)
    hidden_in = draw_hidden_in(jax.random.fold_in(jax.random.fold_in(seeds[11], part), 71), part)
    row_counts = draw_row_counts(jax.random.fold_in(jax.random.fold_in(seeds[11], part), 71), part)
    qkv_new = draw_qkv_new(jax.random.fold_in(jax.random.fold_in(seeds[11], part), 71), part)
    cache_len = draw_cache_len(jax.random.fold_in(jax.random.fold_in(seeds[11], part), 71), part)
    kv_cache = draw_kv_cache(jax.random.fold_in(jax.random.fold_in(seeds[11], part), 71), part)
    w_out = scatter_about(seeds[5], (HEADS * HEAD_DIM, D), (HEADS * HEAD_DIM) ** -0.5, 0.125, ((0, 8),))
    moe_gain = jnp.clip(1.0 + 0.18 * jax.random.normal(seeds[6], (D,), jnp.float32), 0.1, 1.9)
    w_in = scatter_about(seeds[7], (EXPERTS, D, 2, FF), D ** -0.5, 0.125, ((0, 16),))
    w_down = scatter_about(seeds[8], (EXPERTS, FF, D), FF ** -0.5, 0.15625, ((0, 16),))
    route_ids_keys = jax.random.split(jax.random.fold_in(own_keys[9], 1), ROWS // RB)
    route_ids_turns = jax.random.permutation(jax.random.fold_in(own_keys[9], 3), ROWS // RB)
    route_ids = jax.vmap(lambda own, number: shared_out(jax.random.fold_in(own_keys[9], 2), own, number, RB, EXPERTS, TOPK, CAP, 2))(route_ids_keys, route_ids_turns).reshape((ROWS, TOPK))
    route_weight = jnp.clip(0.049804688 + 0.39941406 * jax.random.uniform(own_keys[10], (ROWS, TOPK), jnp.float32) ** level_of(own_keys[10], (ROWS, TOPK), ((0, 16),), -0.2, 0.2), 0.049804688, 0.44921875).astype(jnp.bfloat16)
    return {"hidden_in": hidden_in, "row_counts": row_counts, "qkv_new": qkv_new, "cache_len": cache_len, "kv_cache": kv_cache, "w_out": w_out, "moe_gain": moe_gain, "w_in": w_in, "w_down": w_down, "route_ids": route_ids, "route_weight": route_weight}


epsilon = 1e-06
masked_score = -1e+30

def reference(hidden_in, row_counts, qkv_new, cache_len, kv_cache, w_out, moe_gain, w_in, w_down, route_ids, route_weight):
    head_width = HEADS * HEAD_DIM
    blocks = N_EP * N_REP
    row_index = jnp.arange(ROWS, dtype=jnp.int32)
    block_of = row_index // RB
    counts_row = lax.optimization_barrier(jnp.sum(jnp.where(block_of[:, None] == jnp.arange(blocks, dtype=jnp.int32)[None, :], row_counts[None, :], 0), axis=1))
    is_live = row_index % RB < counts_row
    lengths = cache_len.reshape(ROWS)
    score_scale = 1.0 / math.sqrt(HEAD_DIM)
    fresh_rows = qkv_new.astype(jnp.float32).reshape(ROWS, 3, HEADS, HEAD_DIM)
    queries = fresh_rows[:, 0]
    own_score = lax.optimization_barrier(jnp.sum(queries * fresh_rows[:, 1], axis=2)) * score_scale
    cached = kv_cache.reshape(2, ROWS // RB, RB, L, HEADS, HEAD_DIM)
    group_count = ROWS // RB

    def attend_block(inputs):
        query_rows, key_rows, value_rows, length_rows, own_rows, value_fresh = inputs
        scores = jnp.einsum('bhd,blhd->bhl', query_rows, key_rows.astype(jnp.float32), precision=lax.Precision.HIGHEST) * score_scale
        position = jnp.arange(L, dtype=jnp.int32)
        in_cache = position[None, None, :] < length_rows[:, None, None]
        scores = jnp.where(in_cache, scores, masked_score)
        highest = jnp.maximum(lax.optimization_barrier(jnp.max(scores, axis=2)), own_rows)
        weights = jnp.where(in_cache, jnp.exp(scores - highest[..., None]), 0.0)
        rounded = lax.optimization_barrier(weights.astype(jnp.bfloat16)).astype(jnp.float32)
        own_weight = jnp.exp(own_rows - highest)
        denominator = lax.optimization_barrier(jnp.sum(weights, axis=2)) + own_weight
        summed = jnp.einsum('bhl,blhd->bhd', rounded, value_rows.astype(jnp.float32), precision=lax.Precision.HIGHEST) + own_weight[..., None] * value_fresh
        return summed / denominator[..., None]
    attended = lax.map(attend_block, (queries.reshape(group_count, RB, HEADS, HEAD_DIM), cached[0], cached[1], lengths.reshape(group_count, RB), own_score.reshape(group_count, RB, HEADS), fresh_rows[:, 2].reshape(group_count, RB, HEADS, HEAD_DIM)))
    attended = attended.reshape(ROWS, head_width).astype(jnp.bfloat16)
    attn_out = jnp.dot(attended, w_out, preferred_element_type=jnp.float32)
    residual = (hidden_in.astype(jnp.float32) + attn_out).astype(jnp.bfloat16)
    residual_wide = lax.optimization_barrier(residual).astype(jnp.float32)
    inverse_rms = lax.rsqrt(lax.optimization_barrier(jnp.mean(residual_wide * residual_wide, axis=1)) + epsilon)
    normed = (residual_wide * inverse_rms[:, None] * moe_gain).astype(jnp.bfloat16)
    expert_ids = jnp.arange(EXPERTS, dtype=jnp.int32)
    named_hits = (route_ids[:, :, None] == expert_ids[None, None, :]) & is_live[:, None, None]
    coeffs = lax.optimization_barrier(jnp.sum(jnp.where(named_hits, route_weight.astype(jnp.float32)[:, :, None], 0.0), axis=1))
    chosen = jnp.any(named_hits, axis=1)
    slot_limit = EXPERTS * CAP

    def one_expert(running, expert):
        order_key = jnp.where(chosen[:, expert], row_index, row_index + ROWS)
        picked = jnp.argsort(order_key)[:slot_limit].astype(jnp.int32)
        rows_in = normed[picked]
        weight_in = lax.dynamic_index_in_dim(w_in, expert, 0, keepdims=False).reshape(D, 2 * FF)
        gate_up = jnp.dot(rows_in, weight_in, preferred_element_type=jnp.float32).reshape(slot_limit, 2, FF)
        hidden_units = (jax.nn.silu(gate_up[:, 0]) * gate_up[:, 1]).astype(jnp.bfloat16)
        weight_down = lax.dynamic_index_in_dim(w_down, expert, 0, keepdims=False)
        produced = jnp.dot(hidden_units, weight_down, preferred_element_type=jnp.float32).astype(jnp.bfloat16)
        produced = lax.optimization_barrier(produced).astype(jnp.float32)
        factor = coeffs[picked, expert]
        return (running.at[picked].add(factor[:, None] * produced), None)
    moe_out, _ = lax.scan(one_expert, jnp.zeros((ROWS, D), jnp.float32), expert_ids)
    mixed = jnp.where(is_live[:, None], residual_wide + moe_out, 0.0).astype(jnp.bfloat16)
    return mixed
```

```python
import functools
import math

import jax
import jax.numpy as jnp
from jax import lax
from jax.experimental import pallas as pl
from jax.experimental.pallas import tpu as pltpu
from jax.sharding import PartitionSpec as P

D = 2048
HEAD_DIM = 128
TOPK = 6


epsilon = 1e-06
masked_score = -1e30


def local(
    hidden_in,
    row_counts,
    qkv_new,
    cache_len,
    kv_cache,
    w_out,
    moe_gain,
    w_in,
    w_down,
    route_ids,
    route_weight,
):
    tok_rows, feat_local = hidden_in.shape
    owners = lax.axis_size("ep")
    parts_seq = lax.axis_size("seq")
    width_local = kv_cache.shape[-1]
    heads_local = width_local // HEAD_DIM
    positions = kv_cache.shape[3]
    share_rows = tok_rows // parts_seq
    attend_rows = owners * share_rows
    moved_block = lax.all_to_all(qkv_new, "ep", split_axis=2, concat_axis=0, tiled=True)
    moved_block = moved_block.reshape(owners, tok_rows, 3, width_local)
    heads_block = lax.dynamic_slice_in_dim(
        moved_block, lax.axis_index("seq") * share_rows, share_rows, 1
    )
    heads_block = heads_block.reshape(attend_rows, 3, heads_local, HEAD_DIM)
    queries = heads_block[:, 0]
    key_new = heads_block[:, 1].astype(jnp.float32)
    value_new = heads_block[:, 2].astype(jnp.float32)
    lengths = cache_len.reshape(attend_rows)
    cache_keys = kv_cache[0].reshape(attend_rows, positions, heads_local, HEAD_DIM)
    cache_values = kv_cache[1].reshape(attend_rows, positions, heads_local, HEAD_DIM)
    score_scale = 1.0 / math.sqrt(HEAD_DIM)
    position = jnp.arange(positions, dtype=jnp.int32)
    in_cache = position[None, None, :] < lengths[:, None, None]
    scores = (
        jnp.einsum("nhd,nphd->nhp", queries, cache_keys, preferred_element_type=jnp.float32)
        * score_scale
    )
    scores = jnp.where(in_cache, scores, masked_score)
    own_score = jnp.sum(queries.astype(jnp.float32) * key_new, axis=2) * score_scale
    highest = jnp.maximum(jnp.max(scores, axis=2), own_score)
    weights = jnp.where(in_cache, jnp.exp(scores - highest[..., None]), 0.0)
    partial_sum = jnp.einsum(
        "nhp,nphd->nhd",
        weights.astype(jnp.bfloat16),
        cache_values,
        preferred_element_type=jnp.float32,
    )
    own_weight = jnp.exp(own_score - highest)
    attended = (partial_sum + own_weight[..., None] * value_new) / (
        jnp.sum(weights, axis=2) + own_weight
    )[..., None]
    attended = attended.astype(jnp.bfloat16).reshape(owners, share_rows, width_local)
    attended = lax.all_gather(attended, "seq", axis=1, tiled=True).reshape(
        owners * tok_rows, width_local
    )
    attn_out = lax.psum_scatter(
        jnp.dot(attended, w_out, preferred_element_type=jnp.float32),
        "ep",
        scatter_dimension=0,
        tiled=True,
    )
    residual = (hidden_in.astype(jnp.float32) + attn_out).astype(jnp.bfloat16)
    residual_wide = lax.optimization_barrier(residual).astype(jnp.float32)
    is_live = jnp.arange(tok_rows, dtype=jnp.int32) < row_counts[0]
    expert_total = lax.axis_size(("ep", "rep")) * w_in.shape[0]
    capacity = min(tok_rows, max(2, 2 * tok_rows * TOPK // expert_total))
    pair_count = tok_rows * TOPK
    flat_ids = route_ids.reshape(pair_count)
    pair_hits = (
        flat_ids[:, None] == jnp.arange(expert_total, dtype=jnp.int32)[None, :]
    ) & jnp.repeat(is_live, TOPK)[:, None]
    hit_counts = pair_hits.astype(jnp.int32)
    earlier_hits = jnp.cumsum(hit_counts, axis=0) - hit_counts
    slot_index = jnp.sum(earlier_hits * hit_counts, axis=1)
    target_cell = jnp.where(
        jnp.any(pair_hits, axis=1), flat_ids * capacity + slot_index, -1
    ).reshape(tok_rows, TOPK)
    cell_index = jnp.arange(expert_total * capacity, dtype=jnp.int32)
    cell_hits = target_cell[None, :, :] == cell_index[:, None, None]
    dispatch_rows = jnp.any(cell_hits, axis=2).astype(jnp.bfloat16)
    combine_rows = jnp.sum(
        jnp.where(cell_hits, route_weight.astype(jnp.float32)[None], 0.0), axis=2
    ).astype(jnp.bfloat16)
    full_rows = lax.all_gather(residual, "seq", axis=1, tiled=True)
    rows_wide = full_rows.astype(jnp.float32)
    inverse_rms = lax.rsqrt(jnp.mean(rows_wide * rows_wide, axis=1) + epsilon)
    normed = (rows_wide * inverse_rms[:, None] * moe_gain).astype(jnp.bfloat16)
    outgoing = jnp.dot(dispatch_rows, normed, preferred_element_type=jnp.float32).astype(
        jnp.bfloat16
    )
    outgoing = outgoing.reshape(expert_total, capacity, D)
    arrived = lax.all_to_all(outgoing, ("ep", "rep"), split_axis=0, concat_axis=0, tiled=True)
    sources, slot_count, feature_count = arrived.shape
    flat_rows = arrived.reshape(sources * slot_count, D)
    gate_up = jnp.dot(flat_rows, w_in.reshape(D, -1), preferred_element_type=jnp.float32).reshape(
        sources * slot_count, 2, -1
    )
    hidden_units = (jax.nn.silu(gate_up[:, 0]) * gate_up[:, 1]).astype(jnp.bfloat16)
    down_part = jnp.dot(
        hidden_units, w_down.reshape(-1, D), preferred_element_type=jnp.float32
    ).reshape(sources, slot_count, D)
    summed = lax.psum_scatter(down_part, "seq", scatter_dimension=2, tiled=True).astype(
        jnp.bfloat16
    )
    returned = lax.all_to_all(summed, ("ep", "rep"), split_axis=0, concat_axis=0, tiled=True)
    returned = returned.reshape(expert_total * capacity, feat_local)
    moe_out = lax.dot_general(
        combine_rows, returned, (((0,), (0,)), ((), ())), preferred_element_type=jnp.float32
    )
    mixed = jnp.where(is_live[:, None], residual_wide + moe_out, 0.0).astype(jnp.bfloat16)
    return mixed


LANES = 128
F32 = jnp.float32
BF16 = jnp.bfloat16


def layer_kernel(
    owners,
    qkv_ref,
    lens_ref,
    kv_hbm,
    w_out_ref,
    hidden_ref,
    gain_ref,
    coef_ref,
    live_ref,
    w_in_hbm,
    w_down_hbm,
    out_ref,
    kv_buf,
    q_buf,
    pair_out,
    pair_in,
    col_out,
    col_in,
    total,
    rows_all,
    w_in_buf,
    w_down_buf,
    hidden_buf,
    y_out,
    y_in,
    y_own,
    pair_out2,
    pair_in2,
    col_out2,
    col_in2,
    kv_sem,
    w_sem,
    q_send,
    q_recv,
    pair_send,
    pair_recv,
    col_send,
    col_recv,
    z_send,
    x_send,
    s_send,
    g_recv,
    y_send,
    y_recv,
    pair_send2,
    pair_recv2,
    col_send2,
    col_recv2,
):
    cols = owners // 2
    me = lax.axis_index("ep")
    rep = lax.axis_index("rep")
    mz, mx = me // 2, me % 2
    across = mz * 2 + (1 - mx)
    sister = 1 - rep
    block, width = hidden_ref.shape
    part = kv_buf.shape[-1]
    positions = kv_buf.shape[-2]
    heads = part // HEAD_DIM
    used = heads * block

    def remote(src, dst, send, recv, ep=None, core=None):
        return pltpu.make_async_remote_copy(
            src_ref=src,
            dst_ref=dst,
            send_sem=send,
            recv_sem=recv,
            device_id={"ep": me if ep is None else ep, "rep": rep if core is None else core},
            device_id_type=pl.DeviceIdType.MESH,
        )

    def kv_copy(owner, slot):
        return pltpu.make_async_copy(kv_hbm.at[:, owner], kv_buf.at[slot], kv_sem.at[slot])

    def owner_of(j, s):
        z = (mz + 1 + j) % cols
        return z * 2 + (1 - mx if s == 0 else mx)

    in_copy = pltpu.make_async_copy(w_in_hbm, w_in_buf, w_sem.at[0])
    down_copy = pltpu.make_async_copy(w_down_hbm, w_down_buf, w_sem.at[1])
    kv_copy(owner_of(0, 0), 0).start()
    kv_copy(owner_of(0, 1), 1).start()
    in_copy.start()
    down_copy.start()

    barrier = pltpu.get_barrier_semaphore()
    for i in range(1, owners):
        pl.semaphore_signal(
            barrier,
            inc=1,
            device_id={"ep": (me + i) % owners, "rep": rep},
            device_id_type=pl.DeviceIdType.MESH,
        )
    pl.semaphore_signal(
        barrier, inc=1, device_id={"ep": me, "rep": sister}, device_id_type=pl.DeviceIdType.MESH
    )
    pl.semaphore_wait(barrier, owners)

    def q_part(owner):
        return qkv_ref.at[:, :, pl.ds(pl.multiple_of(owner * part, part), part)]

    @pl.loop(1, owners)
    def _(i):
        to = (me + owners - i) % owners
        remote(q_part(to), q_buf.at[me], q_send.at[to], q_recv.at[me], ep=to).start()

    q_buf[me] = qkv_ref[:, :, pl.ds(pl.multiple_of(me * part, part), part)]

    lane_row = lax.broadcasted_iota(jnp.int32, (positions, LANES), 1) % block
    pos_of = lax.broadcasted_iota(jnp.int32, (positions, LANES), 0)
    head_of = lax.broadcasted_iota(jnp.int32, (block, part), 1) // HEAD_DIM
    row_mod = lax.broadcasted_iota(jnp.int32, (used, positions), 0) % block
    scale = 1.0 / math.sqrt(HEAD_DIM)
    group = 8

    def partial(owner, slot):
        query = q_buf[owner, 0]
        fresh_k = q_buf[owner, 1]
        fresh_v = q_buf[owner, 2].astype(F32)
        zero = jnp.zeros_like(query)
        stack = [jnp.where(head_of == h, query, zero) for h in range(heads)]
        stack += [zero] * (LANES // block - heads)
        queries = jnp.concatenate(stack, axis=0)
        nt = (((1,), (1,)), ((), ()))

        def score_step(g, acc):
            keys = kv_buf[slot, 0, pl.ds(g * group, group)].reshape(group * positions, part)
            got = lax.dot_general(keys, queries, nt, preferred_element_type=F32)
            for r in range(group):
                acc = jnp.where(
                    lane_row == g * group + r, got[r * positions : (r + 1) * positions], acc
                )
            return acc

        scores = lax.fori_loop(
            0, block // group, score_step, jnp.zeros((positions, LANES), F32)
        )
        fresh = lax.dot_general(fresh_k, queries, nt, preferred_element_type=F32)
        diag = lax.broadcasted_iota(jnp.int32, (block, LANES), 0) == (
            lax.broadcasted_iota(jnp.int32, (block, LANES), 1) % block
        )
        own = jnp.sum(jnp.where(diag, fresh, 0.0), axis=0, keepdims=True) * scale
        in_cache = pos_of < lens_ref[owner]
        scores = jnp.where(in_cache, scores * scale, masked_score)
        top = jnp.maximum(jnp.max(scores, axis=0, keepdims=True), own)
        weights = jnp.where(in_cache, jnp.exp(scores - top), 0.0)
        own_w = jnp.exp(own - top)
        den = jnp.sum(weights, axis=0, keepdims=True) + own_w
        own_t = jnp.broadcast_to(own_w, (LANES, LANES)).T
        den_t = jnp.broadcast_to(den, (LANES, LANES)).T
        weights_t = weights.T[:used]

        def value_step(g, acc):
            wide = jnp.concatenate(
                [
                    jnp.where(row_mod == g * group + r, weights_t, 0.0).astype(BF16)
                    for r in range(group)
                ],
                axis=1,
            )
            values = kv_buf[slot, 1, pl.ds(g * group, group)].reshape(group * positions, part)
            return acc + jnp.dot(wide, values, preferred_element_type=F32)

        summed = lax.fori_loop(0, block // group, value_step, jnp.zeros((used, part), F32))
        pieces = []
        for h in range(heads):
            rows = slice(h * block, (h + 1) * block)
            lanes = slice(h * HEAD_DIM, (h + 1) * HEAD_DIM)
            pieces.append((summed[rows, lanes] + own_t[rows] * fresh_v[:, lanes]) / den_t[rows])
        attended = jnp.concatenate(pieces, axis=1).astype(BF16)
        return jnp.dot(attended, w_out_ref[...], preferred_element_type=F32)

    def arrive_q(owner):
        @pl.when(owner != me)
        def _():
            remote(q_part(owner), q_buf.at[owner], q_send.at[owner], q_recv.at[owner], ep=owner).wait_recv()

    def pair_copy(z):
        return remote(pair_out.at[z], pair_in.at[z], pair_send.at[z], pair_recv.at[z], ep=across)

    def col_copy(z, slot):
        return remote(
            col_out.at[z], col_in.at[slot], col_send.at[z], col_recv.at[slot], ep=z * 2 + mx
        )

    @pl.loop(0, cols)
    def _(j):
        z = (mz + 1 + j) % cols
        first, second = owner_of(j, 0), owner_of(j, 1)
        arrive_q(first)
        kv_copy(first, 0).wait()
        pair_out[z] = partial(first, 0).astype(BF16)
        pair_copy(z).start()

        @pl.when(j < cols - 1)
        def _():
            kv_copy(owner_of(j + 1, 0), 0).start()

        arrive_q(second)
        kv_copy(second, 1).wait()
        mine = partial(second, 1)

        @pl.when(j < cols - 1)
        def _():
            kv_copy(owner_of(j + 1, 1), 1).start()

        pair_copy(z).wait_recv()
        mine = mine + pair_in[z].astype(F32)

        @pl.when(j < cols - 1)
        def _():
            col_out[z] = mine.astype(BF16)
            col_copy(z, mz).start()

        @pl.when(j == cols - 1)
        def _():
            total[...] = mine

    for j in range(1, cols):
        z = (mz + j) % cols
        col_copy(z, z).wait_recv()
        total[...] += col_in[z].astype(F32)
    residual = (hidden_ref[...].astype(F32) + total[...]).astype(BF16)
    wide = residual.astype(F32)
    total[...] = wide
    inverse = lax.rsqrt(jnp.mean(wide * wide, axis=1, keepdims=True) + epsilon)
    rows_all[rep, me, :, :width] = (wide * inverse * gain_ref[...]).astype(BF16)
    rows_all[rep, me, :, width:] = coef_ref[...]

    def z_copy(z, e):
        return remote(
            rows_all.at[rep, e], rows_all.at[rep, e], z_send.at[z], g_recv.at[rep, e], ep=z * 2 + mx
        )

    def x_copy(e):
        return remote(
            rows_all.at[rep, e], rows_all.at[rep, e], x_send.at[e], g_recv.at[rep, e], ep=across
        )

    def s_copy(e, side):
        return remote(
            rows_all.at[side, e], rows_all.at[side, e], s_send.at[e], g_recv.at[side, e], core=sister
        )

    for j in range(1, cols):
        z_copy((mz + j) % cols, me).start()
    x_copy(me).start()
    s_copy(me, rep).start()
    for j in range(1, cols):
        e = ((mz + j) % cols) * 2 + mx
        z_copy(e // 2, e).wait_recv()
        x_copy(e).start()
        s_copy(e, rep).start()
    for j in range(cols):
        e = ((mz + j) % cols) * 2 + 1 - mx
        x_copy(e).wait_recv()
        s_copy(e, rep).start()
    in_copy.wait()
    down_copy.wait()

    @pl.loop(0, owners)
    def _(e):
        s_copy(e, sister).wait_recv()

    expert = me * 2 + rep
    tiles = w_in_buf.shape[0]
    half = owners * block
    step = 2 * LANES

    def experts(side, store):
        @pl.loop(0, tiles)
        def _(n):
            rows = rows_all[side, :, :, :width].reshape(half, width)
            both = jnp.dot(rows, w_in_buf[n], preferred_element_type=F32)
            gate, up = both[:, :LANES], both[:, LANES:]
            hidden_buf[:, pl.ds(pl.multiple_of(n * LANES, LANES), LANES)] = (
                gate / (1.0 + jnp.exp(-gate)) * up
            ).astype(BF16)

        coefs = rows_all[side, :, :, width:].reshape(half, LANES).astype(F32)
        lane = lax.broadcasted_iota(jnp.int32, (half, LANES), 1)
        factor = jnp.sum(jnp.where(lane == expert, coefs, 0.0), axis=1, keepdims=True)

        @pl.loop(0, width // step)
        def _(n):
            lanes = pl.ds(pl.multiple_of(n * step, step), step)
            made = jnp.dot(hidden_buf[...], w_down_buf[:, lanes], preferred_element_type=F32)
            store(lanes, (made.astype(BF16).astype(F32) * factor).reshape(owners, block, step))

    def store_out(lanes, v):
        y_out[:, :, lanes] = v.astype(BF16)

    def store_own(lanes, v):
        y_own[:, :, lanes] = v

    experts(sister, store_out)
    y_copy = remote(y_out, y_in, y_send, y_recv, core=sister)
    y_copy.start()
    experts(rep, store_own)
    y_copy.wait()

    def pair_copy2(z):
        return remote(
            pair_out2.at[z], pair_in2.at[z], pair_send2.at[z], pair_recv2.at[z], ep=across
        )

    def col_copy2(z, slot):
        return remote(
            col_out2.at[z], col_in2.at[slot], col_send2.at[z], col_recv2.at[slot], ep=z * 2 + mx
        )

    for j in range(cols):
        z = (mz + 1 + j) % cols
        e = z * 2 + 1 - mx
        pair_out2[z] = (y_own[e] + y_in[e].astype(F32)).astype(BF16)
        pair_copy2(z).start()
    for j in range(cols):
        z = (mz + 1 + j) % cols
        e = z * 2 + mx
        pair_copy2(z).wait_recv()
        mine = y_own[e] + y_in[e].astype(F32) + pair_in2[z].astype(F32)
        if j < cols - 1:
            col_out2[z] = mine.astype(BF16)
            col_copy2(z, mz).start()
        else:
            total[...] += mine
    for j in range(1, cols):
        z = (mz + j) % cols
        col_copy2(z, z).wait_recv()
        total[...] += col_in2[z].astype(F32)
    out_ref[...] = jnp.where(live_ref[:, :1] > 0.0, total[...], 0.0).astype(BF16)

    @pl.loop(1, owners)
    def _(i):
        to = (me + i) % owners
        remote(q_part(to), q_buf.at[me], q_send.at[to], q_recv.at[me], ep=to).wait_send()

    for z in range(cols):
        pair_copy(z).wait_send()
        pair_copy2(z).wait_send()
    for j in range(1, cols):
        z = (mz + j) % cols
        col_copy(z, mz).wait_send()
        col_copy2(z, mz).wait_send()
        z_copy(z, me).wait_send()
    for j in range(cols):
        x_copy(((mz + j) % cols) * 2 + mx).wait_send()

    @pl.loop(0, owners)
    def _(e):
        s_copy(e, rep).wait_send()


def fast_local(
    owners,
    hidden_in,
    row_counts,
    qkv_new,
    cache_len,
    kv_cache,
    w_out,
    moe_gain,
    w_in,
    w_down,
    route_ids,
    route_weight,
):
    block, width = hidden_in.shape
    part = kv_cache.shape[-1]
    positions = kv_cache.shape[3]
    cols = owners // 2
    inner = w_down.shape[1]
    tiles = inner // LANES
    fresh = jnp.transpose(qkv_new, (1, 0, 2))
    lens = jnp.tile(cache_len, (1, LANES // block)).reshape(owners, 1, LANES)
    live = jnp.arange(block, dtype=jnp.int32) < row_counts[0]
    lane = jnp.arange(LANES, dtype=jnp.int32)
    hits = (route_ids[:, :, None] == lane[None, None, :]) & live[:, None, None]
    coef = jnp.sum(jnp.where(hits, route_weight.astype(F32)[:, :, None], 0.0), axis=1).astype(BF16)
    live_wide = jnp.broadcast_to(live[:, None], (block, LANES)).astype(F32)
    w_tiles = jnp.transpose(w_in.reshape(width, 2, tiles, LANES), (2, 0, 1, 3)).reshape(
        tiles, width, 2 * LANES
    )
    vmem = pl.BlockSpec(memory_space=pltpu.VMEM)
    hbm = pl.BlockSpec(memory_space=pl.ANY)
    dma = pltpu.SemaphoreType.DMA
    wide = (cols, block, width)
    return pl.pallas_call(
        functools.partial(layer_kernel, owners),
        out_shape=jax.ShapeDtypeStruct((block, width), BF16),
        in_specs=[vmem, vmem, hbm, vmem, vmem, vmem, vmem, vmem, hbm, hbm],
        out_specs=vmem,
        scratch_shapes=[
            pltpu.VMEM((2, 2, block, positions, part), BF16),
            pltpu.VMEM((owners, 3, block, part), BF16),
            pltpu.VMEM(wide, BF16),
            pltpu.VMEM(wide, BF16),
            pltpu.VMEM(wide, BF16),
            pltpu.VMEM(wide, BF16),
            pltpu.VMEM((block, width), F32),
            pltpu.VMEM((2, owners, block, width + LANES), BF16),
            pltpu.VMEM((tiles, width, 2 * LANES), BF16),
            pltpu.VMEM((inner, width), BF16),
            pltpu.VMEM((owners * block, inner), BF16),
            pltpu.VMEM((owners, block, width), BF16),
            pltpu.VMEM((owners, block, width), BF16),
            pltpu.VMEM((owners, block, width), F32),
            pltpu.VMEM(wide, BF16),
            pltpu.VMEM(wide, BF16),
            pltpu.VMEM(wide, BF16),
            pltpu.VMEM(wide, BF16),
            dma((2,)),
            dma((2,)),
            dma((owners,)),
            dma((owners,)),
            dma((cols,)),
            dma((cols,)),
            dma((cols,)),
            dma((cols,)),
            dma((cols,)),
            dma((owners,)),
            dma((owners,)),
            dma((2, owners)),
            dma(()),
            dma(()),
            dma((cols,)),
            dma((cols,)),
            dma((cols,)),
            dma((cols,)),
        ],
        compiler_params=pltpu.CompilerParams(
            collective_id=0, has_side_effects=True, vmem_limit_bytes=60 * 1024 * 1024
        ),
    )(
        fresh,
        lens,
        kv_cache,
        w_out,
        hidden_in,
        moe_gain.reshape(1, width),
        coef,
        live_wide,
        w_tiles,
        w_down.reshape(inner, width),
    )


def solution(mesh):
    placed = (
        P(("grp", "ep", "rep"), "seq"),
        P(("grp", "ep", "rep")),
        P(("grp", "ep", "rep"), None, None),
        P("grp", ("rep", "seq")),
        P(None, "grp", ("rep", "seq"), None, "ep"),
        P("ep", "seq"),
        P(),
        P(("ep", "rep"), None, None, "seq"),
        P(("ep", "rep"), "seq", None),
        P(("grp", "ep", "rep"), None),
        P(("grp", "ep", "rep"), None),
    )
    sizes = mesh.shape
    owners = sizes["ep"]
    one_step = sizes["seq"] == 1 and sizes["rep"] == 2 and owners % 2 == 0 and owners <= 8
    body = functools.partial(fast_local, owners) if one_step else local
    return jax.shard_map(
        body, mesh=mesh, in_specs=placed, out_specs=P(("grp", "ep", "rep"), "seq"), check_vma=False
    )
```

```python
import functools
import math

import jax
import jax.numpy as jnp
from jax import lax
from jax.experimental import pallas as pl
from jax.experimental.pallas import tpu as pltpu
from jax.sharding import PartitionSpec as P

D = 2048
HEAD_DIM = 128
TOPK = 6


epsilon = 1e-06
masked_score = -1e30


def local(
    hidden_in,
    row_counts,
    qkv_new,
    cache_len,
    kv_cache,
    w_out,
    moe_gain,
    w_in,
    w_down,
    route_ids,
    route_weight,
):
    tok_rows, feat_local = hidden_in.shape
    owners = lax.axis_size("ep")
    parts_seq = lax.axis_size("seq")
    width_local = kv_cache.shape[-1]
    heads_local = width_local // HEAD_DIM
    positions = kv_cache.shape[3]
    share_rows = tok_rows // parts_seq
    attend_rows = owners * share_rows
    moved_block = lax.all_to_all(qkv_new, "ep", split_axis=2, concat_axis=0, tiled=True)
    moved_block = moved_block.reshape(owners, tok_rows, 3, width_local)
    heads_block = lax.dynamic_slice_in_dim(
        moved_block, lax.axis_index("seq") * share_rows, share_rows, 1
    )
    heads_block = heads_block.reshape(attend_rows, 3, heads_local, HEAD_DIM)
    queries = heads_block[:, 0]
    key_new = heads_block[:, 1].astype(jnp.float32)
    value_new = heads_block[:, 2].astype(jnp.float32)
    lengths = cache_len.reshape(attend_rows)
    cache_keys = kv_cache[0].reshape(attend_rows, positions, heads_local, HEAD_DIM)
    cache_values = kv_cache[1].reshape(attend_rows, positions, heads_local, HEAD_DIM)
    score_scale = 1.0 / math.sqrt(HEAD_DIM)
    position = jnp.arange(positions, dtype=jnp.int32)
    in_cache = position[None, None, :] < lengths[:, None, None]
    scores = (
        jnp.einsum("nhd,nphd->nhp", queries, cache_keys, preferred_element_type=jnp.float32)
        * score_scale
    )
    scores = jnp.where(in_cache, scores, masked_score)
    own_score = jnp.sum(queries.astype(jnp.float32) * key_new, axis=2) * score_scale
    highest = jnp.maximum(jnp.max(scores, axis=2), own_score)
    weights = jnp.where(in_cache, jnp.exp(scores - highest[..., None]), 0.0)
    partial_sum = jnp.einsum(
        "nhp,nphd->nhd",
        weights.astype(jnp.bfloat16),
        cache_values,
        preferred_element_type=jnp.float32,
    )
    own_weight = jnp.exp(own_score - highest)
    attended = (partial_sum + own_weight[..., None] * value_new) / (
        jnp.sum(weights, axis=2) + own_weight
    )[..., None]
    attended = attended.astype(jnp.bfloat16).reshape(owners, share_rows, width_local)
    attended = lax.all_gather(attended, "seq", axis=1, tiled=True).reshape(
        owners * tok_rows, width_local
    )
    attn_out = lax.psum_scatter(
        jnp.dot(attended, w_out, preferred_element_type=jnp.float32),
        "ep",
        scatter_dimension=0,
        tiled=True,
    )
    residual = (hidden_in.astype(jnp.float32) + attn_out).astype(jnp.bfloat16)
    residual_wide = lax.optimization_barrier(residual).astype(jnp.float32)
    is_live = jnp.arange(tok_rows, dtype=jnp.int32) < row_counts[0]
    expert_total = lax.axis_size(("ep", "rep")) * w_in.shape[0]
    capacity = min(tok_rows, max(2, 2 * tok_rows * TOPK // expert_total))
    pair_count = tok_rows * TOPK
    flat_ids = route_ids.reshape(pair_count)
    pair_hits = (
        flat_ids[:, None] == jnp.arange(expert_total, dtype=jnp.int32)[None, :]
    ) & jnp.repeat(is_live, TOPK)[:, None]
    hit_counts = pair_hits.astype(jnp.int32)
    earlier_hits = jnp.cumsum(hit_counts, axis=0) - hit_counts
    slot_index = jnp.sum(earlier_hits * hit_counts, axis=1)
    target_cell = jnp.where(
        jnp.any(pair_hits, axis=1), flat_ids * capacity + slot_index, -1
    ).reshape(tok_rows, TOPK)
    cell_index = jnp.arange(expert_total * capacity, dtype=jnp.int32)
    cell_hits = target_cell[None, :, :] == cell_index[:, None, None]
    dispatch_rows = jnp.any(cell_hits, axis=2).astype(jnp.bfloat16)
    combine_rows = jnp.sum(
        jnp.where(cell_hits, route_weight.astype(jnp.float32)[None], 0.0), axis=2
    ).astype(jnp.bfloat16)
    full_rows = lax.all_gather(residual, "seq", axis=1, tiled=True)
    rows_wide = full_rows.astype(jnp.float32)
    inverse_rms = lax.rsqrt(jnp.mean(rows_wide * rows_wide, axis=1) + epsilon)
    normed = (rows_wide * inverse_rms[:, None] * moe_gain).astype(jnp.bfloat16)
    outgoing = jnp.dot(dispatch_rows, normed, preferred_element_type=jnp.float32).astype(
        jnp.bfloat16
    )
    outgoing = outgoing.reshape(expert_total, capacity, D)
    arrived = lax.all_to_all(outgoing, ("ep", "rep"), split_axis=0, concat_axis=0, tiled=True)
    sources, slot_count, feature_count = arrived.shape
    flat_rows = arrived.reshape(sources * slot_count, D)
    gate_up = jnp.dot(flat_rows, w_in.reshape(D, -1), preferred_element_type=jnp.float32).reshape(
        sources * slot_count, 2, -1
    )
    hidden_units = (jax.nn.silu(gate_up[:, 0]) * gate_up[:, 1]).astype(jnp.bfloat16)
    down_part = jnp.dot(
        hidden_units, w_down.reshape(-1, D), preferred_element_type=jnp.float32
    ).reshape(sources, slot_count, D)
    summed = lax.psum_scatter(down_part, "seq", scatter_dimension=2, tiled=True).astype(
        jnp.bfloat16
    )
    returned = lax.all_to_all(summed, ("ep", "rep"), split_axis=0, concat_axis=0, tiled=True)
    returned = returned.reshape(expert_total * capacity, feat_local)
    moe_out = lax.dot_general(
        combine_rows, returned, (((0,), (0,)), ((), ())), preferred_element_type=jnp.float32
    )
    mixed = jnp.where(is_live[:, None], residual_wide + moe_out, 0.0).astype(jnp.bfloat16)
    return mixed


LANES = 128
F32 = jnp.float32
BF16 = jnp.bfloat16


def layer_kernel(
    owners,
    qkv_ref,
    lens_ref,
    kv_hbm,
    w_out_ref,
    hidden_ref,
    gain_ref,
    coef_ref,
    live_ref,
    w_in_hbm,
    w_down_hbm,
    out_ref,
    kv_buf,
    q_buf,
    pair_out,
    pair_in,
    col_out,
    col_in,
    total,
    rows_all,
    w_in_buf,
    w_down_buf,
    hidden_buf,
    y_out,
    y_in,
    y_own,
    pair_out2,
    pair_in2,
    col_out2,
    col_in2,
    kv_sem,
    w_sem,
    q_send,
    q_recv,
    pair_send,
    pair_recv,
    col_send,
    col_recv,
    z_send,
    x_send,
    s_send,
    g_recv,
    y_send,
    y_recv,
    pair_send2,
    pair_recv2,
    col_send2,
    col_recv2,
):
    cols = owners // 2
    me = lax.axis_index("ep")
    rep = lax.axis_index("rep")
    mz, mx = me // 2, me % 2
    across = mz * 2 + (1 - mx)
    sister = 1 - rep
    block, width = hidden_ref.shape
    part = kv_buf.shape[-1]
    positions = kv_buf.shape[-2]
    heads = part // HEAD_DIM
    used = heads * block

    def remote(src, dst, send, recv, ep=None, core=None):
        return pltpu.make_async_remote_copy(
            src_ref=src,
            dst_ref=dst,
            send_sem=send,
            recv_sem=recv,
            device_id={"ep": me if ep is None else ep, "rep": rep if core is None else core},
            device_id_type=pl.DeviceIdType.MESH,
        )

    def kv_copy(owner, slot):
        return pltpu.make_async_copy(kv_hbm.at[:, owner], kv_buf.at[slot], kv_sem.at[slot])

    def owner_of(j, s):
        z = (mz + 1 + j) % cols
        return z * 2 + (1 - mx if s == 0 else mx)

    in_copy = pltpu.make_async_copy(w_in_hbm, w_in_buf, w_sem.at[0])
    down_copy = pltpu.make_async_copy(w_down_hbm, w_down_buf, w_sem.at[1])
    kv_copy(owner_of(0, 0), 0).start()
    kv_copy(owner_of(0, 1), 1).start()
    in_copy.start()
    down_copy.start()

    barrier = pltpu.get_barrier_semaphore()
    for i in range(1, owners):
        pl.semaphore_signal(
            barrier,
            inc=1,
            device_id={"ep": (me + i) % owners, "rep": rep},
            device_id_type=pl.DeviceIdType.MESH,
        )
    pl.semaphore_signal(
        barrier, inc=1, device_id={"ep": me, "rep": sister}, device_id_type=pl.DeviceIdType.MESH
    )
    pl.semaphore_wait(barrier, owners)

    def q_part(owner):
        return qkv_ref.at[:, :, pl.ds(pl.multiple_of(owner * part, part), part)]

    @pl.loop(1, owners)
    def _(i):
        to = (me + owners - i) % owners
        remote(q_part(to), q_buf.at[me], q_send.at[to], q_recv.at[me], ep=to).start()

    q_buf[me] = qkv_ref[:, :, pl.ds(pl.multiple_of(me * part, part), part)]

    lane_row = lax.broadcasted_iota(jnp.int32, (positions, LANES), 1) % block
    pos_of = lax.broadcasted_iota(jnp.int32, (positions, LANES), 0)
    head_of = lax.broadcasted_iota(jnp.int32, (block, part), 1) // HEAD_DIM
    row_mod = lax.broadcasted_iota(jnp.int32, (used, positions), 0) % block
    scale = 1.0 / math.sqrt(HEAD_DIM)
    group = 8

    def partial(owner, slot):
        query = q_buf[owner, 0]
        fresh_k = q_buf[owner, 1]
        fresh_v = q_buf[owner, 2].astype(F32)
        zero = jnp.zeros_like(query)
        stack = [jnp.where(head_of == h, query, zero) for h in range(heads)]
        stack += [zero] * (LANES // block - heads)
        queries = jnp.concatenate(stack, axis=0)
        nt = (((1,), (1,)), ((), ()))

        def score_step(g, acc):
            keys = kv_buf[slot, 0, pl.ds(g * group, group)].reshape(group * positions, part)
            got = lax.dot_general(keys, queries, nt, preferred_element_type=F32)
            for r in range(group):
                acc = jnp.where(
                    lane_row == g * group + r, got[r * positions : (r + 1) * positions], acc
                )
            return acc

        scores = lax.fori_loop(
            0, block // group, score_step, jnp.zeros((positions, LANES), F32)
        )
        fresh = lax.dot_general(fresh_k, queries, nt, preferred_element_type=F32)
        diag = lax.broadcasted_iota(jnp.int32, (block, LANES), 0) == (
            lax.broadcasted_iota(jnp.int32, (block, LANES), 1) % block
        )
        own = jnp.sum(jnp.where(diag, fresh, 0.0), axis=0, keepdims=True) * scale
        in_cache = pos_of < lens_ref[owner]
        scores = jnp.where(in_cache, scores * scale, masked_score)
        top = jnp.maximum(jnp.max(scores, axis=0, keepdims=True), own)
        weights = jnp.where(in_cache, jnp.exp(scores - top), 0.0)
        own_w = jnp.exp(own - top)
        den = jnp.sum(weights, axis=0, keepdims=True) + own_w
        own_t = jnp.broadcast_to(own_w, (LANES, LANES)).T
        den_t = jnp.broadcast_to(den, (LANES, LANES)).T
        weights_t = weights.T[:used]

        def value_step(g, acc):
            wide = jnp.concatenate(
                [
                    jnp.where(row_mod == g * group + r, weights_t, 0.0).astype(BF16)
                    for r in range(group)
                ],
                axis=1,
            )
            values = kv_buf[slot, 1, pl.ds(g * group, group)].reshape(group * positions, part)
            return acc + jnp.dot(wide, values, preferred_element_type=F32)

        summed = lax.fori_loop(0, block // group, value_step, jnp.zeros((used, part), F32))
        pieces = []
        for h in range(heads):
            rows = slice(h * block, (h + 1) * block)
            lanes = slice(h * HEAD_DIM, (h + 1) * HEAD_DIM)
            pieces.append((summed[rows, lanes] + own_t[rows] * fresh_v[:, lanes]) / den_t[rows])
        attended = jnp.concatenate(pieces, axis=1).astype(BF16)
        return jnp.dot(attended, w_out_ref[...], preferred_element_type=F32)

    def arrive_q(owner):
        @pl.when(owner != me)
        def _():
            remote(q_part(owner), q_buf.at[owner], q_send.at[owner], q_recv.at[owner], ep=owner).wait_recv()

    def pair_copy(z):
        return remote(pair_out.at[z], pair_in.at[z], pair_send.at[z], pair_recv.at[z], ep=across)

    def col_copy(z, slot):
        return remote(
            col_out.at[z], col_in.at[slot], col_send.at[z], col_recv.at[slot], ep=z * 2 + mx
        )

    @pl.loop(0, cols)
    def _(j):
        z = (mz + 1 + j) % cols
        first, second = owner_of(j, 0), owner_of(j, 1)
        arrive_q(first)
        kv_copy(first, 0).wait()
        pair_out[z] = partial(first, 0).astype(BF16)
        pair_copy(z).start()

        @pl.when(j < cols - 1)
        def _():
            kv_copy(owner_of(j + 1, 0), 0).start()

        arrive_q(second)
        kv_copy(second, 1).wait()
        mine = partial(second, 1)

        @pl.when(j < cols - 1)
        def _():
            kv_copy(owner_of(j + 1, 1), 1).start()

        pair_copy(z).wait_recv()
        mine = mine + pair_in[z].astype(F32)

        @pl.when(j < cols - 1)
        def _():
            col_out[z] = mine.astype(BF16)
            col_copy(z, mz).start()

        @pl.when(j == cols - 1)
        def _():
            total[...] = mine

    for j in range(1, cols):
        z = (mz + j) % cols
        col_copy(z, z).wait_recv()
        total[...] += col_in[z].astype(F32)
    residual = (hidden_ref[...].astype(F32) + total[...]).astype(BF16)
    wide = residual.astype(F32)
    total[...] = wide
    inverse = lax.rsqrt(jnp.mean(wide * wide, axis=1, keepdims=True) + epsilon)
    rows_all[rep, me, :, :width] = (wide * inverse * gain_ref[...]).astype(BF16)
    rows_all[rep, me, :, width:] = coef_ref[...]

    def z_copy(z, e):
        return remote(
            rows_all.at[rep, e], rows_all.at[rep, e], z_send.at[z], g_recv.at[rep, e], ep=z * 2 + mx
        )

    def x_copy(e):
        return remote(
            rows_all.at[rep, e], rows_all.at[rep, e], x_send.at[e], g_recv.at[rep, e], ep=across
        )

    def s_copy(e, side):
        return remote(
            rows_all.at[side, e], rows_all.at[side, e], s_send.at[e], g_recv.at[side, e], core=sister
        )

    for j in range(1, cols):
        z_copy((mz + j) % cols, me).start()
    x_copy(me).start()
    s_copy(me, rep).start()
    for j in range(1, cols):
        e = ((mz + j) % cols) * 2 + mx
        z_copy(e // 2, e).wait_recv()
        x_copy(e).start()
        s_copy(e, rep).start()
    for j in range(cols):
        e = ((mz + j) % cols) * 2 + 1 - mx
        x_copy(e).wait_recv()
        s_copy(e, rep).start()
    in_copy.wait()
    down_copy.wait()

    @pl.loop(0, owners)
    def _(e):
        s_copy(e, sister).wait_recv()

    expert = me * 2 + rep
    tiles = w_in_buf.shape[2] // LANES
    half = owners * block
    step = 2 * LANES

    def experts(side, store):
        @pl.loop(0, tiles)
        def _(n):
            rows = rows_all[side, :, :, :width].reshape(half, width)
            lanes = pl.ds(pl.multiple_of(n * LANES, LANES), LANES)
            both_w = jnp.concatenate([w_in_buf[0, :, lanes], w_in_buf[1, :, lanes]], axis=1)
            both = jnp.dot(rows, both_w, preferred_element_type=F32)
            gate, up = both[:, :LANES], both[:, LANES:]
            hidden_buf[:, lanes] = (
                gate / (1.0 + jnp.exp(-gate)) * up
            ).astype(BF16)

        coefs = rows_all[side, :, :, width:].reshape(half, LANES).astype(F32)
        lane = lax.broadcasted_iota(jnp.int32, (half, LANES), 1)
        factor = jnp.sum(jnp.where(lane == expert, coefs, 0.0), axis=1, keepdims=True)

        @pl.loop(0, width // step)
        def _(n):
            lanes = pl.ds(pl.multiple_of(n * step, step), step)
            made = jnp.dot(hidden_buf[...], w_down_buf[:, lanes], preferred_element_type=F32)
            store(lanes, (made.astype(BF16).astype(F32) * factor).reshape(owners, block, step))

    def store_out(lanes, v):
        y_out[:, :, lanes] = v.astype(BF16)

    def store_own(lanes, v):
        y_own[:, :, lanes] = v

    experts(sister, store_out)
    y_copy = remote(y_out, y_in, y_send, y_recv, core=sister)
    y_copy.start()
    experts(rep, store_own)
    y_copy.wait()

    def pair_copy2(z):
        return remote(
            pair_out2.at[z], pair_in2.at[z], pair_send2.at[z], pair_recv2.at[z], ep=across
        )

    def col_copy2(z, slot):
        return remote(
            col_out2.at[z], col_in2.at[slot], col_send2.at[z], col_recv2.at[slot], ep=z * 2 + mx
        )

    for j in range(cols):
        z = (mz + 1 + j) % cols
        e = z * 2 + 1 - mx
        pair_out2[z] = (y_own[e] + y_in[e].astype(F32)).astype(BF16)
        pair_copy2(z).start()
    for j in range(cols):
        z = (mz + 1 + j) % cols
        e = z * 2 + mx
        pair_copy2(z).wait_recv()
        mine = y_own[e] + y_in[e].astype(F32) + pair_in2[z].astype(F32)
        if j < cols - 1:
            col_out2[z] = mine.astype(BF16)
            col_copy2(z, mz).start()
        else:
            total[...] += mine
    for j in range(1, cols):
        z = (mz + j) % cols
        col_copy2(z, z).wait_recv()
        total[...] += col_in2[z].astype(F32)
    out_ref[...] = jnp.where(live_ref[:, :1] > 0.0, total[...], 0.0).astype(BF16)

    @pl.loop(1, owners)
    def _(i):
        to = (me + i) % owners
        remote(q_part(to), q_buf.at[me], q_send.at[to], q_recv.at[me], ep=to).wait_send()

    for z in range(cols):
        pair_copy(z).wait_send()
        pair_copy2(z).wait_send()
    for j in range(1, cols):
        z = (mz + j) % cols
        col_copy(z, mz).wait_send()
        col_copy2(z, mz).wait_send()
        z_copy(z, me).wait_send()
    for j in range(cols):
        x_copy(((mz + j) % cols) * 2 + mx).wait_send()

    @pl.loop(0, owners)
    def _(e):
        s_copy(e, rep).wait_send()


def fast_local(
    owners,
    hidden_in,
    row_counts,
    qkv_new,
    cache_len,
    kv_cache,
    w_out,
    moe_gain,
    w_in,
    w_down,
    route_ids,
    route_weight,
):
    block, width = hidden_in.shape
    part = kv_cache.shape[-1]
    positions = kv_cache.shape[3]
    cols = owners // 2
    inner = w_down.shape[1]
    fresh = jnp.transpose(qkv_new, (1, 0, 2))
    lens = jnp.tile(cache_len, (1, LANES // block)).reshape(owners, 1, LANES)
    live = jnp.arange(block, dtype=jnp.int32) < row_counts[0]
    lane = jnp.arange(LANES, dtype=jnp.int32)
    hits = (route_ids[:, :, None] == lane[None, None, :]) & live[:, None, None]
    coef = jnp.sum(jnp.where(hits, route_weight.astype(F32)[:, :, None], 0.0), axis=1).astype(BF16)
    live_wide = jnp.broadcast_to(live[:, None], (block, LANES)).astype(F32)
    w_planes = jnp.transpose(w_in.reshape(width, 2, inner), (1, 0, 2))
    vmem = pl.BlockSpec(memory_space=pltpu.VMEM)
    hbm = pl.BlockSpec(memory_space=pl.ANY)
    dma = pltpu.SemaphoreType.DMA
    wide = (cols, block, width)
    return pl.pallas_call(
        functools.partial(layer_kernel, owners),
        out_shape=jax.ShapeDtypeStruct((block, width), BF16),
        in_specs=[vmem, vmem, hbm, vmem, vmem, vmem, vmem, vmem, hbm, hbm],
        out_specs=vmem,
        scratch_shapes=[
            pltpu.VMEM((2, 2, block, positions, part), BF16),
            pltpu.VMEM((owners, 3, block, part), BF16),
            pltpu.VMEM(wide, BF16),
            pltpu.VMEM(wide, BF16),
            pltpu.VMEM(wide, BF16),
            pltpu.VMEM(wide, BF16),
            pltpu.VMEM((block, width), F32),
            pltpu.VMEM((2, owners, block, width + LANES), BF16),
            pltpu.VMEM((2, width, inner), BF16),
            pltpu.VMEM((inner, width), BF16),
            pltpu.VMEM((owners * block, inner), BF16),
            pltpu.VMEM((owners, block, width), BF16),
            pltpu.VMEM((owners, block, width), BF16),
            pltpu.VMEM((owners, block, width), F32),
            pltpu.VMEM(wide, BF16),
            pltpu.VMEM(wide, BF16),
            pltpu.VMEM(wide, BF16),
            pltpu.VMEM(wide, BF16),
            dma((2,)),
            dma((2,)),
            dma((owners,)),
            dma((owners,)),
            dma((cols,)),
            dma((cols,)),
            dma((cols,)),
            dma((cols,)),
            dma((cols,)),
            dma((owners,)),
            dma((owners,)),
            dma((2, owners)),
            dma(()),
            dma(()),
            dma((cols,)),
            dma((cols,)),
            dma((cols,)),
            dma((cols,)),
        ],
        compiler_params=pltpu.CompilerParams(
            collective_id=0, has_side_effects=True, vmem_limit_bytes=60 * 1024 * 1024
        ),
    )(
        fresh,
        lens,
        kv_cache,
        w_out,
        hidden_in,
        moe_gain.reshape(1, width),
        coef,
        live_wide,
        w_planes,
        w_down.reshape(inner, width),
    )


def solution(mesh):
    placed = (
        P(("grp", "ep", "rep"), "seq"),
        P(("grp", "ep", "rep")),
        P(("grp", "ep", "rep"), None, None),
        P("grp", ("rep", "seq")),
        P(None, "grp", ("rep", "seq"), None, "ep"),
        P("ep", "seq"),
        P(),
        P(("ep", "rep"), None, None, "seq"),
        P(("ep", "rep"), "seq", None),
        P(("grp", "ep", "rep"), None),
        P(("grp", "ep", "rep"), None),
    )
    sizes = mesh.shape
    owners = sizes["ep"]
    one_step = sizes["seq"] == 1 and sizes["rep"] == 2 and owners % 2 == 0 and owners <= 8
    body = functools.partial(fast_local, owners) if one_step else local
    return jax.shard_map(
        body, mesh=mesh, in_specs=placed, out_specs=P(("grp", "ep", "rep"), "seq"), check_vma=False
    )
```

```python
import functools
import math

import jax
import jax.numpy as jnp
from jax import lax
from jax.experimental import pallas as pl
from jax.experimental.pallas import tpu as pltpu
from jax.sharding import PartitionSpec as P

D = 2048
HEAD_DIM = 128
TOPK = 6


epsilon = 1e-06
masked_score = -1e30


def local(
    hidden_in,
    row_counts,
    qkv_new,
    cache_len,
    kv_cache,
    w_out,
    moe_gain,
    w_in,
    w_down,
    route_ids,
    route_weight,
):
    tok_rows, feat_local = hidden_in.shape
    owners = lax.axis_size("ep")
    parts_seq = lax.axis_size("seq")
    width_local = kv_cache.shape[-1]
    heads_local = width_local // HEAD_DIM
    positions = kv_cache.shape[3]
    share_rows = tok_rows // parts_seq
    attend_rows = owners * share_rows
    moved_block = lax.all_to_all(qkv_new, "ep", split_axis=2, concat_axis=0, tiled=True)
    moved_block = moved_block.reshape(owners, tok_rows, 3, width_local)
    heads_block = lax.dynamic_slice_in_dim(
        moved_block, lax.axis_index("seq") * share_rows, share_rows, 1
    )
    heads_block = heads_block.reshape(attend_rows, 3, heads_local, HEAD_DIM)
    queries = heads_block[:, 0]
    key_new = heads_block[:, 1].astype(jnp.float32)
    value_new = heads_block[:, 2].astype(jnp.float32)
    lengths = cache_len.reshape(attend_rows)
    cache_keys = kv_cache[0].reshape(attend_rows, positions, heads_local, HEAD_DIM)
    cache_values = kv_cache[1].reshape(attend_rows, positions, heads_local, HEAD_DIM)
    score_scale = 1.0 / math.sqrt(HEAD_DIM)
    position = jnp.arange(positions, dtype=jnp.int32)
    in_cache = position[None, None, :] < lengths[:, None, None]
    scores = (
        jnp.einsum("nhd,nphd->nhp", queries, cache_keys, preferred_element_type=jnp.float32)
        * score_scale
    )
    scores = jnp.where(in_cache, scores, masked_score)
    own_score = jnp.sum(queries.astype(jnp.float32) * key_new, axis=2) * score_scale
    highest = jnp.maximum(jnp.max(scores, axis=2), own_score)
    weights = jnp.where(in_cache, jnp.exp(scores - highest[..., None]), 0.0)
    partial_sum = jnp.einsum(
        "nhp,nphd->nhd",
        weights.astype(jnp.bfloat16),
        cache_values,
        preferred_element_type=jnp.float32,
    )
    own_weight = jnp.exp(own_score - highest)
    attended = (partial_sum + own_weight[..., None] * value_new) / (
        jnp.sum(weights, axis=2) + own_weight
    )[..., None]
    attended = attended.astype(jnp.bfloat16).reshape(owners, share_rows, width_local)
    attended = lax.all_gather(attended, "seq", axis=1, tiled=True).reshape(
        owners * tok_rows, width_local
    )
    attn_out = lax.psum_scatter(
        jnp.dot(attended, w_out, preferred_element_type=jnp.float32),
        "ep",
        scatter_dimension=0,
        tiled=True,
    )
    residual = (hidden_in.astype(jnp.float32) + attn_out).astype(jnp.bfloat16)
    residual_wide = lax.optimization_barrier(residual).astype(jnp.float32)
    is_live = jnp.arange(tok_rows, dtype=jnp.int32) < row_counts[0]
    expert_total = lax.axis_size(("ep", "rep")) * w_in.shape[0]
    capacity = min(tok_rows, max(2, 2 * tok_rows * TOPK // expert_total))
    pair_count = tok_rows * TOPK
    flat_ids = route_ids.reshape(pair_count)
    pair_hits = (
        flat_ids[:, None] == jnp.arange(expert_total, dtype=jnp.int32)[None, :]
    ) & jnp.repeat(is_live, TOPK)[:, None]
    hit_counts = pair_hits.astype(jnp.int32)
    earlier_hits = jnp.cumsum(hit_counts, axis=0) - hit_counts
    slot_index = jnp.sum(earlier_hits * hit_counts, axis=1)
    target_cell = jnp.where(
        jnp.any(pair_hits, axis=1), flat_ids * capacity + slot_index, -1
    ).reshape(tok_rows, TOPK)
    cell_index = jnp.arange(expert_total * capacity, dtype=jnp.int32)
    cell_hits = target_cell[None, :, :] == cell_index[:, None, None]
    dispatch_rows = jnp.any(cell_hits, axis=2).astype(jnp.bfloat16)
    combine_rows = jnp.sum(
        jnp.where(cell_hits, route_weight.astype(jnp.float32)[None], 0.0), axis=2
    ).astype(jnp.bfloat16)
    full_rows = lax.all_gather(residual, "seq", axis=1, tiled=True)
    rows_wide = full_rows.astype(jnp.float32)
    inverse_rms = lax.rsqrt(jnp.mean(rows_wide * rows_wide, axis=1) + epsilon)
    normed = (rows_wide * inverse_rms[:, None] * moe_gain).astype(jnp.bfloat16)
    outgoing = jnp.dot(dispatch_rows, normed, preferred_element_type=jnp.float32).astype(
        jnp.bfloat16
    )
    outgoing = outgoing.reshape(expert_total, capacity, D)
    arrived = lax.all_to_all(outgoing, ("ep", "rep"), split_axis=0, concat_axis=0, tiled=True)
    sources, slot_count, feature_count = arrived.shape
    flat_rows = arrived.reshape(sources * slot_count, D)
    gate_up = jnp.dot(flat_rows, w_in.reshape(D, -1), preferred_element_type=jnp.float32).reshape(
        sources * slot_count, 2, -1
    )
    hidden_units = (jax.nn.silu(gate_up[:, 0]) * gate_up[:, 1]).astype(jnp.bfloat16)
    down_part = jnp.dot(
        hidden_units, w_down.reshape(-1, D), preferred_element_type=jnp.float32
    ).reshape(sources, slot_count, D)
    summed = lax.psum_scatter(down_part, "seq", scatter_dimension=2, tiled=True).astype(
        jnp.bfloat16
    )
    returned = lax.all_to_all(summed, ("ep", "rep"), split_axis=0, concat_axis=0, tiled=True)
    returned = returned.reshape(expert_total * capacity, feat_local)
    moe_out = lax.dot_general(
        combine_rows, returned, (((0,), (0,)), ((), ())), preferred_element_type=jnp.float32
    )
    mixed = jnp.where(is_live[:, None], residual_wide + moe_out, 0.0).astype(jnp.bfloat16)
    return mixed


LANES = 128
F32 = jnp.float32
BF16 = jnp.bfloat16


def layer_kernel(
    owners,
    qkv_ref,
    lens_ref,
    kv_hbm,
    w_out_ref,
    hidden_ref,
    gain_ref,
    ids_ref,
    gate_ref,
    count_ref,
    w_in_hbm,
    w_down_hbm,
    out_ref,
    kv_buf,
    q_buf,
    pair_out,
    pair_in,
    col_out,
    col_in,
    total,
    rows_all,
    w_in_buf,
    w_down_buf,
    hidden_buf,
    y_all,
    y_in,
    pair_out2,
    pair_in2,
    col_out2,
    col_in2,
    kv_sem,
    w_sem,
    q_send,
    q_recv,
    pair_send,
    pair_recv,
    col_send,
    col_recv,
    z_send,
    x_send,
    s_send,
    g_recv,
    y_send,
    y_recv,
    pair_send2,
    pair_recv2,
    col_send2,
    col_recv2,
):
    cols = owners // 2
    me = lax.axis_index("ep")
    rep = lax.axis_index("rep")
    mz, mx = me // 2, me % 2
    across = mz * 2 + (1 - mx)
    sister = 1 - rep
    block, width = hidden_ref.shape
    part = kv_buf.shape[-1]
    positions = kv_buf.shape[-2]
    heads = part // HEAD_DIM
    used = heads * block

    def remote(src, dst, send, recv, ep=None, core=None):
        return pltpu.make_async_remote_copy(
            src_ref=src,
            dst_ref=dst,
            send_sem=send,
            recv_sem=recv,
            device_id={"ep": me if ep is None else ep, "rep": rep if core is None else core},
            device_id_type=pl.DeviceIdType.MESH,
        )

    def kv_copy(owner, slot):
        return pltpu.make_async_copy(kv_hbm.at[:, owner], kv_buf.at[slot], kv_sem.at[slot])

    def owner_of(j, s):
        z = (mz + 1 + j) % cols
        return z * 2 + (1 - mx if s == 0 else mx)

    in_copy = pltpu.make_async_copy(w_in_hbm, w_in_buf, w_sem.at[0])
    down_copy = pltpu.make_async_copy(w_down_hbm, w_down_buf, w_sem.at[1])
    kv_copy(owner_of(0, 0), 0).start()
    kv_copy(owner_of(0, 1), 1).start()
    in_copy.start()
    down_copy.start()

    barrier = pltpu.get_barrier_semaphore()
    for i in range(1, owners):
        pl.semaphore_signal(
            barrier,
            inc=1,
            device_id={"ep": (me + i) % owners, "rep": rep},
            device_id_type=pl.DeviceIdType.MESH,
        )
    pl.semaphore_signal(
        barrier, inc=1, device_id={"ep": me, "rep": sister}, device_id_type=pl.DeviceIdType.MESH
    )
    pl.semaphore_wait(barrier, owners)

    def q_part(owner):
        return qkv_ref.at[:, :, pl.ds(pl.multiple_of(owner * part, part), part)]

    @pl.loop(1, owners)
    def _(i):
        to = (me + owners - i) % owners
        remote(q_part(to), q_buf.at[me], q_send.at[to], q_recv.at[me], ep=to).start()

    q_buf[me] = qkv_ref[:, :, pl.ds(pl.multiple_of(me * part, part), part)]

    is_live = lax.broadcasted_iota(jnp.int32, (block, 1), 0) < count_ref[0]
    lane_id = lax.broadcasted_iota(jnp.int32, (block, LANES), 1)
    gates = gate_ref[...].astype(F32)
    coef = jnp.zeros((block, LANES), F32)
    for k in range(TOPK):
        coef += jnp.where(lane_id == ids_ref[:, k : k + 1], gates[:, k : k + 1], 0.0)
    rows_all[mx, rep, mz, :, width:] = jnp.where(is_live, coef, 0.0).astype(BF16)

    lane_row = lax.broadcasted_iota(jnp.int32, (positions, LANES), 1) % block
    pos_of = lax.broadcasted_iota(jnp.int32, (positions, LANES), 0)
    head_of = lax.broadcasted_iota(jnp.int32, (block, part), 1) // HEAD_DIM
    row_mod = lax.broadcasted_iota(jnp.int32, (used, positions), 0) % block
    scale = 1.0 / math.sqrt(HEAD_DIM)
    group = 8

    def partial(owner, slot):
        query = q_buf[owner, 0]
        fresh_k = q_buf[owner, 1]
        fresh_v = q_buf[owner, 2].astype(F32)
        zero = jnp.zeros_like(query)
        stack = [jnp.where(head_of == h, query, zero) for h in range(heads)]
        stack += [zero] * (LANES // block - heads)
        queries = jnp.concatenate(stack, axis=0)
        nt = (((1,), (1,)), ((), ()))

        def score_step(g, acc):
            keys = kv_buf[slot, 0, pl.ds(g * group, group)].reshape(group * positions, part)
            got = lax.dot_general(keys, queries, nt, preferred_element_type=F32)
            for r in range(group):
                acc = jnp.where(
                    lane_row == g * group + r, got[r * positions : (r + 1) * positions], acc
                )
            return acc

        scores = lax.fori_loop(
            0, block // group, score_step, jnp.zeros((positions, LANES), F32)
        )
        fresh = lax.dot_general(fresh_k, queries, nt, preferred_element_type=F32)
        diag = lax.broadcasted_iota(jnp.int32, (block, LANES), 0) == (
            lax.broadcasted_iota(jnp.int32, (block, LANES), 1) % block
        )
        own = jnp.sum(jnp.where(diag, fresh, 0.0), axis=0, keepdims=True) * scale
        lens = jnp.concatenate([lens_ref[pl.ds(owner, 1), :]] * (LANES // block), axis=1)
        in_cache = pos_of < lens
        scores = jnp.where(in_cache, scores * scale, masked_score)
        top = jnp.maximum(jnp.max(scores, axis=0, keepdims=True), own)
        weights = jnp.where(in_cache, jnp.exp(scores - top), 0.0)
        own_w = jnp.exp(own - top)
        den = jnp.sum(weights, axis=0, keepdims=True) + own_w
        own_t = jnp.broadcast_to(own_w, (LANES, LANES)).T
        den_t = jnp.broadcast_to(den, (LANES, LANES)).T
        weights_t = weights.T[:used]

        def value_step(g, acc):
            wide = jnp.concatenate(
                [
                    jnp.where(row_mod == g * group + r, weights_t, 0.0).astype(BF16)
                    for r in range(group)
                ],
                axis=1,
            )
            values = kv_buf[slot, 1, pl.ds(g * group, group)].reshape(group * positions, part)
            return acc + jnp.dot(wide, values, preferred_element_type=F32)

        summed = lax.fori_loop(0, block // group, value_step, jnp.zeros((used, part), F32))
        pieces = []
        for h in range(heads):
            rows = slice(h * block, (h + 1) * block)
            lanes = slice(h * HEAD_DIM, (h + 1) * HEAD_DIM)
            pieces.append((summed[rows, lanes] + own_t[rows] * fresh_v[:, lanes]) / den_t[rows])
        attended = jnp.concatenate(pieces, axis=1).astype(BF16)
        return jnp.dot(attended, w_out_ref[...], preferred_element_type=F32)

    def arrive_q(owner):
        @pl.when(owner != me)
        def _():
            remote(q_part(owner), q_buf.at[owner], q_send.at[owner], q_recv.at[owner], ep=owner).wait_recv()

    def pair_copy(z):
        return remote(pair_out.at[z], pair_in.at[z], pair_send.at[z], pair_recv.at[z], ep=across)

    def col_copy(z, slot):
        return remote(
            col_out.at[z], col_in.at[slot], col_send.at[z], col_recv.at[slot], ep=z * 2 + mx
        )

    @pl.loop(0, cols)
    def _(j):
        z = (mz + 1 + j) % cols
        first, second = owner_of(j, 0), owner_of(j, 1)
        arrive_q(first)
        kv_copy(first, 0).wait()
        pair_out[z] = partial(first, 0).astype(BF16)
        pair_copy(z).start()

        @pl.when(j < cols - 1)
        def _():
            kv_copy(owner_of(j + 1, 0), 0).start()

        arrive_q(second)
        kv_copy(second, 1).wait()
        mine = partial(second, 1)

        @pl.when(j < cols - 1)
        def _():
            kv_copy(owner_of(j + 1, 1), 1).start()

        pair_copy(z).wait_recv()
        mine = mine + pair_in[z].astype(F32)

        @pl.when(j < cols - 1)
        def _():
            col_out[z] = mine.astype(BF16)
            col_copy(z, mz).start()

        @pl.when(j == cols - 1)
        def _():
            total[...] = mine

    for j in range(1, cols):
        z = (mz + j) % cols
        col_copy(z, z).wait_recv()
        total[...] += col_in[z].astype(F32)
    residual = (hidden_ref[...].astype(F32) + total[...]).astype(BF16)
    wide = residual.astype(F32)
    total[...] = wide
    inverse = lax.rsqrt(jnp.mean(wide * wide, axis=1, keepdims=True) + epsilon)
    rows_all[mx, rep, mz, :, :width] = (wide * inverse * gain_ref[...]).astype(BF16)

    def row_copy(e, side, send, ep=None, core=None):
        at = rows_all.at[e % 2, side, e // 2]
        return remote(at, at, send, g_recv.at[e % 2, side, e // 2], ep=ep, core=core)

    def z_copy(z, e):
        return row_copy(e, rep, z_send.at[z], ep=z * 2 + mx)

    def x_copy(e):
        return row_copy(e, rep, x_send.at[e], ep=across)

    def s_copy(e, side):
        return row_copy(e, side, s_send.at[e], core=sister)

    def y_copy(x):
        return remote(y_all.at[x, sister], y_in.at[x], y_send.at[x], y_recv.at[x], core=sister)

    expert = me * 2 + rep
    tiles = w_in_buf.shape[2] // LANES
    half = owners * block
    step = 2 * LANES

    def experts(x):
        @pl.loop(0, tiles)
        def _(n):
            rows = rows_all[x, :, :, :, :width].reshape(half, width)
            lanes = pl.ds(pl.multiple_of(n * LANES, LANES), LANES)
            both_w = jnp.concatenate([w_in_buf[0, :, lanes], w_in_buf[1, :, lanes]], axis=1)
            both = jnp.dot(rows, both_w, preferred_element_type=F32)
            gate, up = both[:, :LANES], both[:, LANES:]
            hidden_buf[:, lanes] = (gate / (1.0 + jnp.exp(-gate)) * up).astype(BF16)

        coefs = rows_all[x, :, :, :, width:].reshape(half, LANES).astype(F32)
        lane = lax.broadcasted_iota(jnp.int32, (half, LANES), 1)
        factor = jnp.sum(jnp.where(lane == expert, coefs, 0.0), axis=1, keepdims=True)

        @pl.loop(0, width // step)
        def _(n):
            lanes = pl.ds(pl.multiple_of(n * step, step), step)
            made = jnp.dot(hidden_buf[...], w_down_buf[:, lanes], preferred_element_type=F32)
            made = made.astype(BF16).astype(F32) * factor
            y_all[x, :, :, :, lanes] = made.astype(BF16).reshape(2, cols, block, step)

    for j in range(1, cols):
        z_copy((mz + j) % cols, me).start()
    x_copy(me).start()
    s_copy(me, rep).start()
    for j in range(1, cols):
        e = ((mz + j) % cols) * 2 + mx
        z_copy(e // 2, e).wait_recv()
        x_copy(e).start()
        s_copy(e, rep).start()
    in_copy.wait()
    down_copy.wait()
    for z in range(cols):
        s_copy(z * 2 + mx, sister).wait_recv()
    experts(mx)
    y_copy(mx).start()
    for j in range(cols):
        e = ((mz + j) % cols) * 2 + 1 - mx
        x_copy(e).wait_recv()
        s_copy(e, rep).start()
    for z in range(cols):
        s_copy(z * 2 + 1 - mx, sister).wait_recv()
    experts(1 - mx)
    y_copy(1 - mx).start()
    y_copy(1 - mx).wait_recv()

    def pair_copy2(z):
        return remote(
            pair_out2.at[z], pair_in2.at[z], pair_send2.at[z], pair_recv2.at[z], ep=across
        )

    def col_copy2(z, slot):
        return remote(
            col_out2.at[z], col_in2.at[slot], col_send2.at[z], col_recv2.at[slot], ep=z * 2 + mx
        )

    for j in range(cols):
        z = (mz + 1 + j) % cols
        made = y_all[1 - mx, rep, z].astype(F32) + y_in[1 - mx, z].astype(F32)
        pair_out2[z] = made.astype(BF16)
        pair_copy2(z).start()
    y_copy(mx).wait_recv()
    for j in range(cols):
        z = (mz + 1 + j) % cols
        made = y_all[mx, rep, z].astype(F32) + y_in[mx, z].astype(F32)
        pair_copy2(z).wait_recv()
        mine = made + pair_in2[z].astype(F32)
        if j < cols - 1:
            col_out2[z] = mine.astype(BF16)
            col_copy2(z, mz).start()
        else:
            total[...] += mine
    for j in range(1, cols):
        z = (mz + j) % cols
        col_copy2(z, z).wait_recv()
        total[...] += col_in2[z].astype(F32)
    out_ref[...] = jnp.where(is_live, total[...], 0.0).astype(BF16)

    @pl.loop(1, owners)
    def _(i):
        to = (me + i) % owners
        remote(q_part(to), q_buf.at[me], q_send.at[to], q_recv.at[me], ep=to).wait_send()

    for x in range(2):
        y_copy(x).wait_send()
    for z in range(cols):
        pair_copy(z).wait_send()
        pair_copy2(z).wait_send()
    for j in range(1, cols):
        z = (mz + j) % cols
        col_copy(z, mz).wait_send()
        col_copy2(z, mz).wait_send()
        z_copy(z, me).wait_send()
    for j in range(cols):
        x_copy(((mz + j) % cols) * 2 + mx).wait_send()

    @pl.loop(0, owners)
    def _(e):
        s_copy(e, rep).wait_send()


def fast_local(
    owners,
    hidden_in,
    row_counts,
    qkv_new,
    cache_len,
    kv_cache,
    w_out,
    moe_gain,
    w_in,
    w_down,
    route_ids,
    route_weight,
):
    block, width = hidden_in.shape
    part = kv_cache.shape[-1]
    positions = kv_cache.shape[3]
    cols = owners // 2
    inner = w_down.shape[1]
    fresh = jnp.transpose(qkv_new, (1, 0, 2))
    w_planes = jnp.transpose(w_in.reshape(width, 2, inner), (1, 0, 2))
    vmem = pl.BlockSpec(memory_space=pltpu.VMEM)
    hbm = pl.BlockSpec(memory_space=pl.ANY)
    smem = pl.BlockSpec(memory_space=pltpu.SMEM)
    dma = pltpu.SemaphoreType.DMA
    wide = (cols, block, width)
    return pl.pallas_call(
        functools.partial(layer_kernel, owners),
        out_shape=jax.ShapeDtypeStruct((block, width), BF16),
        in_specs=[vmem, vmem, hbm, vmem, vmem, vmem, vmem, vmem, smem, hbm, hbm],
        out_specs=vmem,
        scratch_shapes=[
            pltpu.VMEM((2, 2, block, positions, part), BF16),
            pltpu.VMEM((owners, 3, block, part), BF16),
            pltpu.VMEM(wide, BF16),
            pltpu.VMEM(wide, BF16),
            pltpu.VMEM(wide, BF16),
            pltpu.VMEM(wide, BF16),
            pltpu.VMEM((block, width), F32),
            pltpu.VMEM((2, 2, cols, block, width + LANES), BF16),
            pltpu.VMEM((2, width, inner), BF16),
            pltpu.VMEM((inner, width), BF16),
            pltpu.VMEM((owners * block, inner), BF16),
            pltpu.VMEM((2, 2, cols, block, width), BF16),
            pltpu.VMEM((2, cols, block, width), BF16),
            pltpu.VMEM(wide, BF16),
            pltpu.VMEM(wide, BF16),
            pltpu.VMEM(wide, BF16),
            pltpu.VMEM(wide, BF16),
            dma((2,)),
            dma((2,)),
            dma((owners,)),
            dma((owners,)),
            dma((cols,)),
            dma((cols,)),
            dma((cols,)),
            dma((cols,)),
            dma((cols,)),
            dma((owners,)),
            dma((owners,)),
            dma((2, 2, cols)),
            dma((2,)),
            dma((2,)),
            dma((cols,)),
            dma((cols,)),
            dma((cols,)),
            dma((cols,)),
        ],
        compiler_params=pltpu.CompilerParams(
            collective_id=0, has_side_effects=True, vmem_limit_bytes=60 * 1024 * 1024
        ),
    )(
        fresh,
        cache_len,
        kv_cache,
        w_out,
        hidden_in,
        moe_gain.reshape(1, width),
        route_ids,
        route_weight,
        row_counts,
        w_planes,
        w_down.reshape(inner, width),
    )


def solution(mesh):
    placed = (
        P(("grp", "ep", "rep"), "seq"),
        P(("grp", "ep", "rep")),
        P(("grp", "ep", "rep"), None, None),
        P("grp", ("rep", "seq")),
        P(None, "grp", ("rep", "seq"), None, "ep"),
        P("ep", "seq"),
        P(),
        P(("ep", "rep"), None, None, "seq"),
        P(("ep", "rep"), "seq", None),
        P(("grp", "ep", "rep"), None),
        P(("grp", "ep", "rep"), None),
    )
    sizes = mesh.shape
    owners = sizes["ep"]
    one_step = sizes["seq"] == 1 and sizes["rep"] == 2 and owners % 2 == 0 and owners <= 8
    body = functools.partial(fast_local, owners) if one_step else local
    return jax.shard_map(
        body, mesh=mesh, in_specs=placed, out_specs=P(("grp", "ep", "rep"), "seq"), check_vma=False
    )
```

```python
import functools
import math

import jax
import jax.numpy as jnp
from jax import lax
from jax.experimental import pallas as pl
from jax.experimental.pallas import tpu as pltpu
from jax.sharding import PartitionSpec as P

D = 2048
HEAD_DIM = 128
TOPK = 6


epsilon = 1e-06
masked_score = -1e30


def local(
    hidden_in,
    row_counts,
    qkv_new,
    cache_len,
    kv_cache,
    w_out,
    moe_gain,
    w_in,
    w_down,
    route_ids,
    route_weight,
):
    tok_rows, feat_local = hidden_in.shape
    owners = lax.axis_size("ep")
    parts_seq = lax.axis_size("seq")
    width_local = kv_cache.shape[-1]
    heads_local = width_local // HEAD_DIM
    positions = kv_cache.shape[3]
    share_rows = tok_rows // parts_seq
    attend_rows = owners * share_rows
    moved_block = lax.all_to_all(qkv_new, "ep", split_axis=2, concat_axis=0, tiled=True)
    moved_block = moved_block.reshape(owners, tok_rows, 3, width_local)
    heads_block = lax.dynamic_slice_in_dim(
        moved_block, lax.axis_index("seq") * share_rows, share_rows, 1
    )
    heads_block = heads_block.reshape(attend_rows, 3, heads_local, HEAD_DIM)
    queries = heads_block[:, 0]
    key_new = heads_block[:, 1].astype(jnp.float32)
    value_new = heads_block[:, 2].astype(jnp.float32)
    lengths = cache_len.reshape(attend_rows)
    cache_keys = kv_cache[0].reshape(attend_rows, positions, heads_local, HEAD_DIM)
    cache_values = kv_cache[1].reshape(attend_rows, positions, heads_local, HEAD_DIM)
    score_scale = 1.0 / math.sqrt(HEAD_DIM)
    position = jnp.arange(positions, dtype=jnp.int32)
    in_cache = position[None, None, :] < lengths[:, None, None]
    scores = (
        jnp.einsum("nhd,nphd->nhp", queries, cache_keys, preferred_element_type=jnp.float32)
        * score_scale
    )
    scores = jnp.where(in_cache, scores, masked_score)
    own_score = jnp.sum(queries.astype(jnp.float32) * key_new, axis=2) * score_scale
    highest = jnp.maximum(jnp.max(scores, axis=2), own_score)
    weights = jnp.where(in_cache, jnp.exp(scores - highest[..., None]), 0.0)
    partial_sum = jnp.einsum(
        "nhp,nphd->nhd",
        weights.astype(jnp.bfloat16),
        cache_values,
        preferred_element_type=jnp.float32,
    )
    own_weight = jnp.exp(own_score - highest)
    attended = (partial_sum + own_weight[..., None] * value_new) / (
        jnp.sum(weights, axis=2) + own_weight
    )[..., None]
    attended = attended.astype(jnp.bfloat16).reshape(owners, share_rows, width_local)
    attended = lax.all_gather(attended, "seq", axis=1, tiled=True).reshape(
        owners * tok_rows, width_local
    )
    attn_out = lax.psum_scatter(
        jnp.dot(attended, w_out, preferred_element_type=jnp.float32),
        "ep",
        scatter_dimension=0,
        tiled=True,
    )
    residual = (hidden_in.astype(jnp.float32) + attn_out).astype(jnp.bfloat16)
    residual_wide = lax.optimization_barrier(residual).astype(jnp.float32)
    is_live = jnp.arange(tok_rows, dtype=jnp.int32) < row_counts[0]
    expert_total = lax.axis_size(("ep", "rep")) * w_in.shape[0]
    capacity = min(tok_rows, max(2, 2 * tok_rows * TOPK // expert_total))
    pair_count = tok_rows * TOPK
    flat_ids = route_ids.reshape(pair_count)
    pair_hits = (
        flat_ids[:, None] == jnp.arange(expert_total, dtype=jnp.int32)[None, :]
    ) & jnp.repeat(is_live, TOPK)[:, None]
    hit_counts = pair_hits.astype(jnp.int32)
    earlier_hits = jnp.cumsum(hit_counts, axis=0) - hit_counts
    slot_index = jnp.sum(earlier_hits * hit_counts, axis=1)
    target_cell = jnp.where(
        jnp.any(pair_hits, axis=1), flat_ids * capacity + slot_index, -1
    ).reshape(tok_rows, TOPK)
    cell_index = jnp.arange(expert_total * capacity, dtype=jnp.int32)
    cell_hits = target_cell[None, :, :] == cell_index[:, None, None]
    dispatch_rows = jnp.any(cell_hits, axis=2).astype(jnp.bfloat16)
    combine_rows = jnp.sum(
        jnp.where(cell_hits, route_weight.astype(jnp.float32)[None], 0.0), axis=2
    ).astype(jnp.bfloat16)
    full_rows = lax.all_gather(residual, "seq", axis=1, tiled=True)
    rows_wide = full_rows.astype(jnp.float32)
    inverse_rms = lax.rsqrt(jnp.mean(rows_wide * rows_wide, axis=1) + epsilon)
    normed = (rows_wide * inverse_rms[:, None] * moe_gain).astype(jnp.bfloat16)
    outgoing = jnp.dot(dispatch_rows, normed, preferred_element_type=jnp.float32).astype(
        jnp.bfloat16
    )
    outgoing = outgoing.reshape(expert_total, capacity, D)
    arrived = lax.all_to_all(outgoing, ("ep", "rep"), split_axis=0, concat_axis=0, tiled=True)
    sources, slot_count, feature_count = arrived.shape
    flat_rows = arrived.reshape(sources * slot_count, D)
    gate_up = jnp.dot(flat_rows, w_in.reshape(D, -1), preferred_element_type=jnp.float32).reshape(
        sources * slot_count, 2, -1
    )
    hidden_units = (jax.nn.silu(gate_up[:, 0]) * gate_up[:, 1]).astype(jnp.bfloat16)
    down_part = jnp.dot(
        hidden_units, w_down.reshape(-1, D), preferred_element_type=jnp.float32
    ).reshape(sources, slot_count, D)
    summed = lax.psum_scatter(down_part, "seq", scatter_dimension=2, tiled=True).astype(
        jnp.bfloat16
    )
    returned = lax.all_to_all(summed, ("ep", "rep"), split_axis=0, concat_axis=0, tiled=True)
    returned = returned.reshape(expert_total * capacity, feat_local)
    moe_out = lax.dot_general(
        combine_rows, returned, (((0,), (0,)), ((), ())), preferred_element_type=jnp.float32
    )
    mixed = jnp.where(is_live[:, None], residual_wide + moe_out, 0.0).astype(jnp.bfloat16)
    return mixed


LANES = 128
F32 = jnp.float32
BF16 = jnp.bfloat16


def layer_kernel(
    owners,
    qkv_ref,
    lens_ref,
    kv_hbm,
    w_out_ref,
    hidden_ref,
    gain_ref,
    ids_ref,
    gate_ref,
    count_ref,
    w_in_hbm,
    w_down_hbm,
    out_ref,
    kv_buf,
    q_buf,
    pair_out,
    pair_in,
    col_out,
    col_in,
    total,
    rows_all,
    w_in_buf,
    w_down_buf,
    hidden_buf,
    y_all,
    y_in,
    pair_out2,
    pair_in2,
    col_out2,
    col_in2,
    kv_sem,
    w_sem,
    q_send,
    q_recv,
    pair_send,
    pair_recv,
    col_send,
    col_recv,
    z_send,
    x_send,
    s_send,
    g_recv,
    y_send,
    y_recv,
    pair_send2,
    pair_recv2,
    col_send2,
    col_recv2,
):
    cols = owners // 2
    me = lax.axis_index("ep")
    rep = lax.axis_index("rep")
    mz, mx = me // 2, me % 2
    across = mz * 2 + (1 - mx)
    sister = 1 - rep
    block, width = hidden_ref.shape
    part = kv_buf.shape[-1]
    positions = kv_buf.shape[-2]
    heads = part // HEAD_DIM
    used = heads * block

    def remote(src, dst, send, recv, ep=None, core=None):
        return pltpu.make_async_remote_copy(
            src_ref=src,
            dst_ref=dst,
            send_sem=send,
            recv_sem=recv,
            device_id={"ep": me if ep is None else ep, "rep": rep if core is None else core},
            device_id_type=pl.DeviceIdType.MESH,
        )

    def kv_copy(owner, slot):
        return pltpu.make_async_copy(kv_hbm.at[:, owner], kv_buf.at[slot], kv_sem.at[slot])

    def owner_of(j, s):
        z = (mz + 1 + j) % cols
        return z * 2 + (1 - mx if s == 0 else mx)

    in_copy = pltpu.make_async_copy(w_in_hbm, w_in_buf, w_sem.at[0])
    down_copy = pltpu.make_async_copy(w_down_hbm, w_down_buf, w_sem.at[1])
    kv_copy(owner_of(0, 0), 0).start()
    kv_copy(owner_of(0, 1), 1).start()
    in_copy.start()
    down_copy.start()

    barrier = pltpu.get_barrier_semaphore()
    for i in range(1, owners):
        pl.semaphore_signal(
            barrier,
            inc=1,
            device_id={"ep": (me + i) % owners, "rep": rep},
            device_id_type=pl.DeviceIdType.MESH,
        )
    pl.semaphore_signal(
        barrier, inc=1, device_id={"ep": me, "rep": sister}, device_id_type=pl.DeviceIdType.MESH
    )
    pl.semaphore_wait(barrier, owners)

    def q_part(owner):
        return qkv_ref.at[:, :, pl.ds(pl.multiple_of(owner * part, part), part)]

    @pl.loop(1, owners)
    def _(i):
        to = (me + owners - i) % owners
        remote(q_part(to), q_buf.at[me], q_send.at[to], q_recv.at[me], ep=to).start()

    q_buf[me] = qkv_ref[:, :, pl.ds(pl.multiple_of(me * part, part), part)]

    is_live = lax.broadcasted_iota(jnp.int32, (block, 1), 0) < count_ref[0]
    expert_id = lax.broadcasted_iota(jnp.int32, (LANES, LANES), 0)
    gates = gate_ref[...].astype(F32)
    ids = jnp.concatenate([ids_ref[...]] * (LANES // block), axis=1)
    gates = jnp.concatenate([gates] * (LANES // block), axis=1)
    coef = jnp.zeros((LANES, LANES), F32)
    for k in range(TOPK):
        coef += jnp.where(expert_id == ids[k : k + 1], gates[k : k + 1], 0.0)
    coef = coef.T[:block]
    rows_all[mx, rep, mz, :, width:] = jnp.where(is_live, coef, 0.0).astype(BF16)

    lane_row = lax.broadcasted_iota(jnp.int32, (1, LANES), 1) % block
    pos_of = lax.broadcasted_iota(jnp.int32, (positions, LANES), 0)
    head_of = lax.broadcasted_iota(jnp.int32, (block, part), 1) // HEAD_DIM
    row_mod = lax.broadcasted_iota(jnp.int32, (used, positions), 0) % block
    scale = 1.0 / math.sqrt(HEAD_DIM)
    group = 8

    def partial(owner, slot):
        query = q_buf[owner, 0]
        fresh_k = q_buf[owner, 1]
        fresh_v = q_buf[owner, 2].astype(F32)
        zero = jnp.zeros_like(query)
        stack = [jnp.where(head_of == h, query, zero) for h in range(heads)]
        stack += [zero] * (LANES // block - heads)
        queries = jnp.concatenate(stack, axis=0)
        nt = (((1,), (1,)), ((), ()))

        def score_step(g, acc):
            keys = kv_buf[slot, 0, pl.ds(g * group, group)].reshape(group * positions, part)
            got = lax.dot_general(keys, queries, nt, preferred_element_type=F32)
            for r in range(group):
                acc = jnp.where(
                    lane_row == g * group + r, got[r * positions : (r + 1) * positions], acc
                )
            return acc

        scores = lax.fori_loop(
            0, block // group, score_step, jnp.zeros((positions, LANES), F32)
        )
        fresh = lax.dot_general(fresh_k, queries, nt, preferred_element_type=F32)
        diag = lax.broadcasted_iota(jnp.int32, (block, LANES), 0) == (
            lax.broadcasted_iota(jnp.int32, (block, LANES), 1) % block
        )
        own = jnp.sum(jnp.where(diag, fresh, 0.0), axis=0, keepdims=True) * scale
        lens = jnp.concatenate([lens_ref[pl.ds(owner, 1), :]] * (LANES // block), axis=1)
        in_cache = pos_of < lens
        scores = jnp.where(in_cache, scores * scale, masked_score)
        top = jnp.maximum(jnp.max(scores, axis=0, keepdims=True), own)
        weights = jnp.where(in_cache, jnp.exp(scores - top), 0.0)
        own_w = jnp.exp(own - top)
        den = jnp.sum(weights, axis=0, keepdims=True) + own_w
        own_t = jnp.broadcast_to(own_w, (LANES, LANES)).T
        den_t = jnp.broadcast_to(den, (LANES, LANES)).T
        weights_t = weights.T[:used]

        def value_step(g, acc):
            wide = jnp.concatenate(
                [
                    jnp.where(row_mod == g * group + r, weights_t, 0.0).astype(BF16)
                    for r in range(group)
                ],
                axis=1,
            )
            values = kv_buf[slot, 1, pl.ds(g * group, group)].reshape(group * positions, part)
            return acc + jnp.dot(wide, values, preferred_element_type=F32)

        summed = lax.fori_loop(0, block // group, value_step, jnp.zeros((used, part), F32))
        pieces = []
        for h in range(heads):
            rows = slice(h * block, (h + 1) * block)
            lanes = slice(h * HEAD_DIM, (h + 1) * HEAD_DIM)
            pieces.append((summed[rows, lanes] + own_t[rows] * fresh_v[:, lanes]) / den_t[rows])
        attended = jnp.concatenate(pieces, axis=1).astype(BF16)
        return jnp.dot(attended, w_out_ref[...], preferred_element_type=F32)

    def arrive_q(owner):
        @pl.when(owner != me)
        def _():
            remote(q_part(owner), q_buf.at[owner], q_send.at[owner], q_recv.at[owner], ep=owner).wait_recv()

    def pair_copy(z):
        return remote(pair_out.at[z], pair_in.at[z], pair_send.at[z], pair_recv.at[z], ep=across)

    def col_copy(z, slot):
        return remote(
            col_out.at[z], col_in.at[slot], col_send.at[z], col_recv.at[slot], ep=z * 2 + mx
        )

    @pl.loop(0, cols)
    def _(j):
        z = (mz + 1 + j) % cols
        first, second = owner_of(j, 0), owner_of(j, 1)
        arrive_q(first)
        kv_copy(first, 0).wait()
        pair_out[z] = partial(first, 0).astype(BF16)
        pair_copy(z).start()

        @pl.when(j < cols - 1)
        def _():
            kv_copy(owner_of(j + 1, 0), 0).start()

        arrive_q(second)
        kv_copy(second, 1).wait()
        mine = partial(second, 1)

        @pl.when(j < cols - 1)
        def _():
            kv_copy(owner_of(j + 1, 1), 1).start()

        pair_copy(z).wait_recv()
        mine = mine + pair_in[z].astype(F32)

        @pl.when(j < cols - 1)
        def _():
            col_out[z] = mine.astype(BF16)
            col_copy(z, mz).start()

        @pl.when(j == cols - 1)
        def _():
            total[...] = mine

    for j in range(1, cols):
        z = (mz + j) % cols
        col_copy(z, z).wait_recv()
        total[...] += col_in[z].astype(F32)
    residual = (hidden_ref[...].astype(F32) + total[...]).astype(BF16)
    wide = residual.astype(F32)
    total[...] = wide
    inverse = lax.rsqrt(jnp.mean(wide * wide, axis=1, keepdims=True) + epsilon)
    rows_all[mx, rep, mz, :, :width] = (wide * inverse * gain_ref[...]).astype(BF16)

    def row_copy(e, side, send, ep=None, core=None):
        at = rows_all.at[e % 2, side, e // 2]
        return remote(at, at, send, g_recv.at[e % 2, side, e // 2], ep=ep, core=core)

    def z_copy(z, e):
        return row_copy(e, rep, z_send.at[z], ep=z * 2 + mx)

    def x_copy(e):
        return row_copy(e, rep, x_send.at[e], ep=across)

    def s_copy(e, side):
        return row_copy(e, side, s_send.at[e], core=sister)

    def y_copy(x):
        return remote(y_all.at[x, sister], y_in.at[x], y_send.at[x], y_recv.at[x], core=sister)

    expert = me * 2 + rep
    tiles = w_in_buf.shape[2] // LANES
    half = owners * block
    step = 2 * LANES

    def experts(x):
        @pl.loop(0, tiles)
        def _(n):
            rows = rows_all[x, :, :, :, :width].reshape(half, width)
            lanes = pl.ds(pl.multiple_of(n * LANES, LANES), LANES)
            both_w = jnp.concatenate([w_in_buf[0, :, lanes], w_in_buf[1, :, lanes]], axis=1)
            both = jnp.dot(rows, both_w, preferred_element_type=F32)
            gate, up = both[:, :LANES], both[:, LANES:]
            hidden_buf[:, lanes] = (gate / (1.0 + jnp.exp(-gate)) * up).astype(BF16)

        coefs = rows_all[x, :, :, :, width:].reshape(half, LANES).astype(F32)
        lane = lax.broadcasted_iota(jnp.int32, (half, LANES), 1)
        factor = jnp.sum(jnp.where(lane == expert, coefs, 0.0), axis=1, keepdims=True)

        @pl.loop(0, width // step)
        def _(n):
            lanes = pl.ds(pl.multiple_of(n * step, step), step)
            made = jnp.dot(hidden_buf[...], w_down_buf[:, lanes], preferred_element_type=F32)
            made = made.astype(BF16).astype(F32) * factor
            y_all[x, :, :, :, lanes] = made.astype(BF16).reshape(2, cols, block, step)

    for j in range(1, cols):
        z_copy((mz + j) % cols, me).start()
    x_copy(me).start()
    s_copy(me, rep).start()
    for j in range(1, cols):
        e = ((mz + j) % cols) * 2 + mx
        z_copy(e // 2, e).wait_recv()
        x_copy(e).start()
        s_copy(e, rep).start()
    in_copy.wait()
    down_copy.wait()
    for z in range(cols):
        s_copy(z * 2 + mx, sister).wait_recv()
    experts(mx)
    y_copy(mx).start()
    for j in range(cols):
        e = ((mz + j) % cols) * 2 + 1 - mx
        x_copy(e).wait_recv()
        s_copy(e, rep).start()
    for z in range(cols):
        s_copy(z * 2 + 1 - mx, sister).wait_recv()
    experts(1 - mx)
    y_copy(1 - mx).start()
    y_copy(1 - mx).wait_recv()

    def pair_copy2(z):
        return remote(
            pair_out2.at[z], pair_in2.at[z], pair_send2.at[z], pair_recv2.at[z], ep=across
        )

    def col_copy2(z, slot):
        return remote(
            col_out2.at[z], col_in2.at[slot], col_send2.at[z], col_recv2.at[slot], ep=z * 2 + mx
        )

    for j in range(cols):
        z = (mz + 1 + j) % cols
        made = y_all[1 - mx, rep, z].astype(F32) + y_in[1 - mx, z].astype(F32)
        pair_out2[z] = made.astype(BF16)
        pair_copy2(z).start()
    y_copy(mx).wait_recv()
    for j in range(cols):
        z = (mz + 1 + j) % cols
        made = y_all[mx, rep, z].astype(F32) + y_in[mx, z].astype(F32)
        pair_copy2(z).wait_recv()
        mine = made + pair_in2[z].astype(F32)
        if j < cols - 1:
            col_out2[z] = mine.astype(BF16)
            col_copy2(z, mz).start()
        else:
            total[...] += mine
    for j in range(1, cols):
        z = (mz + j) % cols
        col_copy2(z, z).wait_recv()
        total[...] += col_in2[z].astype(F32)
    out_ref[...] = jnp.where(is_live, total[...], 0.0).astype(BF16)

    @pl.loop(1, owners)
    def _(i):
        to = (me + i) % owners
        remote(q_part(to), q_buf.at[me], q_send.at[to], q_recv.at[me], ep=to).wait_send()

    for x in range(2):
        y_copy(x).wait_send()
    for z in range(cols):
        pair_copy(z).wait_send()
        pair_copy2(z).wait_send()
    for j in range(1, cols):
        z = (mz + j) % cols
        col_copy(z, mz).wait_send()
        col_copy2(z, mz).wait_send()
        z_copy(z, me).wait_send()
    for j in range(cols):
        x_copy(((mz + j) % cols) * 2 + mx).wait_send()

    @pl.loop(0, owners)
    def _(e):
        s_copy(e, rep).wait_send()


def fast_local(
    owners,
    hidden_in,
    row_counts,
    qkv_new,
    cache_len,
    kv_cache,
    w_out,
    moe_gain,
    w_in,
    w_down,
    route_ids,
    route_weight,
):
    block, width = hidden_in.shape
    part = kv_cache.shape[-1]
    positions = kv_cache.shape[3]
    cols = owners // 2
    inner = w_down.shape[1]
    fresh = jnp.transpose(qkv_new, (1, 0, 2))
    w_planes = jnp.transpose(w_in.reshape(width, 2, inner), (1, 0, 2))
    vmem = pl.BlockSpec(memory_space=pltpu.VMEM)
    hbm = pl.BlockSpec(memory_space=pl.ANY)
    smem = pl.BlockSpec(memory_space=pltpu.SMEM)
    dma = pltpu.SemaphoreType.DMA
    wide = (cols, block, width)
    return pl.pallas_call(
        functools.partial(layer_kernel, owners),
        out_shape=jax.ShapeDtypeStruct((block, width), BF16),
        in_specs=[vmem, vmem, hbm, vmem, vmem, vmem, vmem, vmem, smem, hbm, hbm],
        out_specs=vmem,
        scratch_shapes=[
            pltpu.VMEM((2, 2, block, positions, part), BF16),
            pltpu.VMEM((owners, 3, block, part), BF16),
            pltpu.VMEM(wide, BF16),
            pltpu.VMEM(wide, BF16),
            pltpu.VMEM(wide, BF16),
            pltpu.VMEM(wide, BF16),
            pltpu.VMEM((block, width), F32),
            pltpu.VMEM((2, 2, cols, block, width + LANES), BF16),
            pltpu.VMEM((2, width, inner), BF16),
            pltpu.VMEM((inner, width), BF16),
            pltpu.VMEM((owners * block, inner), BF16),
            pltpu.VMEM((2, 2, cols, block, width), BF16),
            pltpu.VMEM((2, cols, block, width), BF16),
            pltpu.VMEM(wide, BF16),
            pltpu.VMEM(wide, BF16),
            pltpu.VMEM(wide, BF16),
            pltpu.VMEM(wide, BF16),
            dma((2,)),
            dma((2,)),
            dma((owners,)),
            dma((owners,)),
            dma((cols,)),
            dma((cols,)),
            dma((cols,)),
            dma((cols,)),
            dma((cols,)),
            dma((owners,)),
            dma((owners,)),
            dma((2, 2, cols)),
            dma((2,)),
            dma((2,)),
            dma((cols,)),
            dma((cols,)),
            dma((cols,)),
            dma((cols,)),
        ],
        compiler_params=pltpu.CompilerParams(
            collective_id=0, has_side_effects=True, vmem_limit_bytes=60 * 1024 * 1024
        ),
    )(
        fresh,
        cache_len,
        kv_cache,
        w_out,
        hidden_in,
        moe_gain.reshape(1, width),
        route_ids.T,
        route_weight.T,
        row_counts,
        w_planes,
        w_down.reshape(inner, width),
    )


def solution(mesh):
    placed = (
        P(("grp", "ep", "rep"), "seq"),
        P(("grp", "ep", "rep")),
        P(("grp", "ep", "rep"), None, None),
        P("grp", ("rep", "seq")),
        P(None, "grp", ("rep", "seq"), None, "ep"),
        P("ep", "seq"),
        P(),
        P(("ep", "rep"), None, None, "seq"),
        P(("ep", "rep"), "seq", None),
        P(("grp", "ep", "rep"), None),
        P(("grp", "ep", "rep"), None),
    )
    sizes = mesh.shape
    owners = sizes["ep"]
    one_step = sizes["seq"] == 1 and sizes["rep"] == 2 and owners % 2 == 0 and owners <= 8
    body = functools.partial(fast_local, owners) if one_step else local
    return jax.shard_map(
        body, mesh=mesh, in_specs=placed, out_specs=P(("grp", "ep", "rep"), "seq"), check_vma=False
    )
```
